128 devices in a mesh: seq: 16 (over y, x), dp: 8 (over z, core).
Axes of the slice: x: 4, y: 4, z: 4, core: 2. Of those that a mesh axis runs over, the one named last changes fastest.
Arguments:
- points: bfloat16 [8, 16384, 256], P('dp', 'seq'), may hold values from -6 to 6
- targets: int32 [8, 16384], P('dp', 'seq'), may hold values from 0 to 16383, as said below
- cotangent: bfloat16 [8, 16384, 256], P('dp', 'seq'), may hold values from -6 to 6
- w_qkv: bfloat16 [256, 768], replicated
- w_out: bfloat16 [256, 256], replicated, may hold values from -0.375 to 0.375
- w_up: bfloat16 [256, 1024], replicated, may hold values from -0.375 to 0.375
- w_down: bfloat16 [1024, 256], replicated, may hold values from -0.1875 to 0.1875
Outputs:
- result: bfloat16 [8, 16384, 256], P('dp', 'seq')
- grad_points: bfloat16 [8, 16384, 256], P('dp', 'seq')
- grad_qkv: float32 [256, 768], replicated
- grad_out: float32 [256, 256], replicated
- grad_up: float32 [256, 1024], replicated
- grad_down: float32 [1024, 256], replicated
The draws below stay inside these ranges and needn't reach their ends.
Inputs may be any that keep to these rules, and one draw needn't show every extreme that they name: In each tile, targets is a permutation of the tile's positions. With owner = target // 1024, the points held by one index of seq send at most 128 points to any one owner, and exactly 128 to one owner.
All inputs are finite; a program needn't handle non-finite values.
Results may differ from the reference program's by a relative error of at most 0.035.
The reference program's roundings to bfloat16 on the way count: a program that leaves them out, or rounds other values in their place, can miss the bound.
Values may be sent and summed in bfloat16 or wider, within the bound.
A program may use at most 64 MiB of HBM per device.

```python
import math
import jax
import jax.numpy as jnp
from jax import lax

C = 256
HEADS = 16
PATCH = 1024
FF = 1024
ROWS = 1024
POINTS = 16384
TILES = 8
N_SEQ = 16


def shuffle_rows(member_key):
    return jax.random.permutation(member_key, ROWS).astype(jnp.int32)


def tile_targets(tile_key):
    peer_count = N_SEQ
    row_count = ROWS
    slot_room = 2 * row_count // peer_count
    ordering = jax.random.permutation(jax.random.fold_in(tile_key, 1), peer_count).astype(jnp.int32)
    rank_of = jnp.zeros((peer_count,), jnp.int32).at[ordering].set(jnp.arange(peer_count, dtype=jnp.int32))
    half_count = (peer_count - 2) // 2
    spread = jax.random.randint(jax.random.fold_in(tile_key, 2), (half_count,), 0, row_count // (2 * peer_count) + 1).astype(jnp.int32)
    baseline = row_count // peer_count
    weights = jnp.concatenate([jnp.array([slot_room, 0], jnp.int32), baseline + spread, baseline - spread])
    weights = weights[jax.random.permutation(jax.random.fold_in(tile_key, 3), peer_count)]
    offsets = (rank_of[None, :] - rank_of[:, None]) % peer_count
    counts = weights[offsets]
    inclusive = jnp.cumsum(counts, axis=1)
    exclusive = inclusive - counts
    column_start = jnp.cumsum(counts, axis=0) - counts
    within = jax.vmap(shuffle_rows)(jax.random.split(jax.random.fold_in(tile_key, 4), peer_count))
    positions = jnp.arange(row_count, dtype=jnp.int32)

    def source_rows(source, source_key):
        owner = jnp.sum((inclusive[source][None, :] <= positions[:, None]).astype(jnp.int32), axis=1)
        ranking = positions - exclusive[source][owner]
        local_place = column_start[source][owner] + ranking
        final = owner * row_count + within[owner, local_place]
        shuffled = jax.random.permutation(source_key, row_count).astype(jnp.int32)
        return jnp.zeros((row_count,), jnp.int32).at[shuffled].set(final)
    sources = jnp.arange(peer_count, dtype=jnp.int32)
    result = jax.vmap(source_rows)(sources, jax.random.split(jax.random.fold_in(tile_key, 5), peer_count))
    return result.reshape(-1)


def draw_targets(key, part):
    return jax.vmap(tile_targets)(jax.random.split(key, TILES)).astype(jnp.int32)


def draw_w_qkv(key, part):
    base = jax.random.normal(key, (C, 3 * C), jnp.float32) * C ** (-0.5)
    return base.astype(jnp.bfloat16)


def block_levels(own_key, shape, cuts, least, top_value):
    factor_of, own = 1.0, jax.random.fold_in(own_key, 6)
    for axis_at, shards_of in cuts:
        draws = jnp.exp(jax.random.uniform(jax.random.fold_in(own, axis_at), (shards_of,), jnp.float32, least / len(cuts), top_value / len(cuts)))
        factor_of = factor_of * jnp.repeat(draws, shape[axis_at] // shards_of).reshape([-1 if axis == axis_at else 1 for axis in range(len(shape))])
    return factor_of


def noise(own_key, shape, width, limit, shards=(), kind=jnp.bfloat16):
    factor_of = block_levels(own_key, shape, shards, -0.22, 0.18) if shards else 1.0
    entries = jax.random.normal(own_key, shape, jnp.float32) * width * factor_of
    return jnp.minimum(jnp.maximum(entries, -limit), limit).astype(kind)


def setup_inputs(seed: int = 0) -> dict:
    key_list = jax.random.split(jax.random.key(seed), 8)
    return {
        "points": noise(key_list[0], (TILES, POINTS, C), 1.0, 6.0, ((0, 8), (1, 16))),
        "targets": draw_targets(jax.random.fold_in(key_list[7], 71), 0),
        "cotangent": noise(key_list[2], (TILES, POINTS, C), 1.0, 6.0, ((0, 8), (1, 16))),
        "w_qkv": draw_w_qkv(jax.random.fold_in(key_list[7], 71), 0),
        "w_out": noise(key_list[4], (C, C), C ** -0.5, 0.375),
        "w_up": noise(key_list[5], (C, FF), C ** -0.5, 0.375),
        "w_down": noise(key_list[6], (FF, C), FF ** -0.5, 0.1875),
    }


EPS = 1e-05
GELU_A = 0.7978845608028654
GELU_B = 0.044715

def normalize(values):
    center = lax.optimization_barrier(jnp.mean(values, axis=-1, keepdims=True))
    shifted = values - center
    inverse_std = lax.rsqrt(lax.optimization_barrier(jnp.mean(shifted * shifted, axis=-1, keepdims=True)) + EPS)
    return (shifted * inverse_std, inverse_std)

def norm_back(normed, inverse_std, upstream):
    return inverse_std * (upstream - lax.optimization_barrier(jnp.mean(upstream, axis=-1, keepdims=True)) - normed * lax.optimization_barrier(jnp.mean(upstream * normed, axis=-1, keepdims=True)))

def gelu_pair(inputs):
    tangent = jnp.tanh(GELU_A * (inputs + GELU_B * inputs * inputs * inputs))
    outputs = 0.5 * inputs * (1.0 + tangent)
    slopes = 0.5 * (1.0 + tangent) + 0.5 * inputs * (1.0 - tangent * tangent) * GELU_A * (1.0 + 3.0 * GELU_B * inputs * inputs)
    return (outputs, slopes)

def contract_rows(left, right):
    return lax.dot_general(left, right, (((0,), (0,)), ((), ())), preferred_element_type=jnp.float32)

def contract_last(left, right):
    return lax.dot_general(left, right, (((1,), (1,)), ((), ())), preferred_element_type=jnp.float32)

def split_heads(packed, heads):
    row_count = packed.shape[0]
    head_size = packed.shape[1] // (3 * heads)
    shaped = packed.reshape(row_count // PATCH, PATCH, 3, heads, head_size)
    return shaped.transpose(2, 0, 3, 1, 4).reshape(3, row_count // PATCH * heads, PATCH, head_size)

def split_single(packed, heads):
    row_count = packed.shape[0]
    head_size = packed.shape[1] // heads
    shaped = packed.reshape(row_count // PATCH, PATCH, heads, head_size)
    return shaped.transpose(0, 2, 1, 3).reshape(row_count // PATCH * heads, PATCH, head_size)

def merge_heads(stacked, row_count, heads):
    head_size = stacked.shape[-1]
    shaped = stacked.reshape(row_count // PATCH, heads, PATCH, head_size)
    return shaped.transpose(0, 2, 1, 3).reshape(row_count, heads * head_size)

def merge_triple(stacked, row_count, heads):
    head_size = stacked.shape[-1]
    shaped = stacked.reshape(row_count // PATCH, heads, 3, PATCH, head_size)
    return shaped.transpose(0, 3, 2, 1, 4).reshape(row_count, 3 * heads * head_size)

def head_probs(queries, keys_head):
    factor = queries.shape[-1] ** (-0.5)
    scores = jnp.dot(queries, keys_head.T, preferred_element_type=jnp.float32) * factor
    scores = scores - lax.optimization_barrier(jnp.max(scores, axis=-1, keepdims=True))
    raised = jnp.exp(scores)
    return raised / lax.optimization_barrier(jnp.sum(raised, axis=-1, keepdims=True))

def head_forward(members):
    queries, keys_head, values_head = members
    weights_soft = head_probs(queries, keys_head).astype(jnp.bfloat16)
    return jnp.dot(weights_soft, values_head, preferred_element_type=jnp.float32).astype(jnp.bfloat16)

def head_backward(members):
    queries, keys_head, values_head, outputs, upstream = members
    factor = queries.shape[-1] ** (-0.5)
    weights_soft = head_probs(queries, keys_head)
    rounded = weights_soft.astype(jnp.bfloat16)
    grad_values = jnp.dot(rounded.T, upstream, preferred_element_type=jnp.float32)
    grad_weights = jnp.dot(upstream, values_head.T, preferred_element_type=jnp.float32)
    row_inner = lax.optimization_barrier(jnp.sum(upstream.astype(jnp.float32) * outputs.astype(jnp.float32), axis=-1, keepdims=True))
    grad_scores = (weights_soft * (grad_weights - row_inner)).astype(jnp.bfloat16)
    grad_queries = jnp.dot(grad_scores, keys_head, preferred_element_type=jnp.float32) * factor
    grad_keys = jnp.dot(grad_scores.T, queries, preferred_element_type=jnp.float32) * factor
    return jnp.stack([grad_queries, grad_keys, grad_values]).astype(jnp.bfloat16)

def attend(packed, heads):
    pieces = split_heads(packed, heads)
    outputs = lax.map(head_forward, (pieces[0], pieces[1], pieces[2]))
    return merge_heads(outputs, packed.shape[0], heads)

def attend_back(packed, attended, upstream, heads):
    pieces = split_heads(packed, heads)
    out_items = split_single(attended, heads)
    grad_items = split_single(upstream, heads)
    gradients = lax.map(head_backward, (pieces[0], pieces[1], pieces[2], out_items, grad_items))
    return merge_triple(gradients, packed.shape[0], heads)

def reference(points, targets, cotangent, w_qkv, w_out, w_up, w_down):

    def one_tile(members):
        tile_points, tile_places, tile_grad = members
        row_count = tile_points.shape[0]
        features = tile_points.astype(jnp.float32)
        normed_first, inverse_first = normalize(features)
        first_rows = normed_first.astype(jnp.bfloat16)
        projected = jnp.dot(first_rows, w_qkv, preferred_element_type=jnp.float32).astype(jnp.bfloat16)
        inverse = jnp.zeros((row_count,), jnp.int32).at[tile_places.astype(jnp.int32)].set(jnp.arange(row_count, dtype=jnp.int32))
        ordered = projected[inverse]
        attended = attend(ordered, HEADS)
        restored = attended[tile_places]
        hidden = features + jnp.dot(restored, w_out, preferred_element_type=jnp.float32)
        normed_second, inverse_second = normalize(hidden)
        second_rows = normed_second.astype(jnp.bfloat16)
        expanded = jnp.dot(second_rows, w_up, preferred_element_type=jnp.float32)
        activated, slopes = gelu_pair(expanded)
        activated = activated.astype(jnp.bfloat16)
        result = (hidden + jnp.dot(activated, w_down, preferred_element_type=jnp.float32)).astype(jnp.bfloat16)
        grad_active = contract_last(tile_grad, w_down)
        grad_expand = (grad_active * slopes).astype(jnp.bfloat16)
        grad_second = contract_last(grad_expand, w_up)
        grad_hidden = tile_grad.astype(jnp.float32) + norm_back(normed_second, inverse_second, grad_second)
        hidden_rows = grad_hidden.astype(jnp.bfloat16)
        grad_attended = contract_last(hidden_rows, w_out).astype(jnp.bfloat16)
        grad_ordered = attend_back(ordered, attended, grad_attended[inverse], HEADS)
        grad_projected = grad_ordered[tile_places]
        grad_first = contract_last(grad_projected, w_qkv).astype(jnp.bfloat16)
        grad_input = (grad_hidden + norm_back(normed_first, inverse_first, grad_first.astype(jnp.float32))).astype(jnp.bfloat16)
        return (result, grad_input, contract_rows(first_rows, grad_projected), contract_rows(restored, hidden_rows), contract_rows(second_rows, grad_expand), contract_rows(activated, tile_grad))
    gathered = lax.map(one_tile, (points, targets, cotangent))
    factor = 1.0 / math.sqrt(TILES * POINTS)
    return (gathered[0], gathered[1], lax.optimization_barrier(jnp.sum(gathered[2], axis=0)) * factor, lax.optimization_barrier(jnp.sum(gathered[3], axis=0)) * factor, lax.optimization_barrier(jnp.sum(gathered[4], axis=0)) * factor, lax.optimization_barrier(jnp.sum(gathered[5], axis=0)) * factor)
```

```python
import math

import jax
import jax.numpy as jnp
from jax import lax
from jax.experimental import pallas as pl
from jax.experimental.pallas import tpu as pltpu
from jax.sharding import PartitionSpec as P

BF = jnp.bfloat16
F32 = jnp.float32
C = 256
HEADS = 16
DH = 16
FF = 1024
ROWS = 1024
PEERS = 16
ROOM = 128
SLOTS = PEERS * ROOM
BLK = 256
NB = ROWS // BLK
EPS = 1e-05
GELU_A = 0.7978845608028654
GELU_B = 0.044715


def dot(left, right):
    return lax.dot_general(left, right, (((1,), (0,)), ((), ())), preferred_element_type=F32)


def dot_nt(left, right):
    return lax.dot_general(left, right, (((1,), (1,)), ((), ())), preferred_element_type=F32)


def iota(shape, axis):
    return lax.broadcasted_iota(jnp.int32, shape, axis)


def one_hot(cond):
    return jnp.where(cond, 1.0, 0.0).astype(BF)


def transpose_bf(values):
    return values.astype(F32).T.astype(BF)


def normalize(values):
    center = jnp.mean(values, axis=-1, keepdims=True)
    shifted = values - center
    inverse_std = lax.rsqrt(jnp.mean(shifted * shifted, axis=-1, keepdims=True) + EPS)
    return shifted * inverse_std, inverse_std


def norm_back(normed, inverse_std, upstream):
    return inverse_std * (
        upstream
        - jnp.mean(upstream, axis=-1, keepdims=True)
        - normed * jnp.mean(upstream * normed, axis=-1, keepdims=True)
    )


def gelu_pair(inputs):
    square = inputs * inputs
    tangent = jnp.tanh(GELU_A * (inputs + GELU_B * square * inputs))
    half = 0.5 * (1.0 + tangent)
    slopes = half + 0.5 * inputs * (1.0 - tangent * tangent) * GELU_A * (
        1.0 + 3.0 * GELU_B * square
    )
    return inputs * half, slopes


def column_of(row):
    return jnp.broadcast_to(row, (128, 128)).T[:, 0:1]


def slot_rows(targets):
    owner = lax.shift_right_logical(targets, 10)
    local = jnp.bitwise_and(targets, 1023)
    marks = iota((PEERS, ROWS), 0) == owner
    before = one_hot(iota((ROWS, ROWS), 0) < iota((ROWS, ROWS), 1))
    counts = dot(one_hot(marks), before)
    rank = jnp.sum(jnp.where(marks, counts, 0.0), axis=0, keepdims=True)
    slot = owner * ROOM + rank.astype(jnp.int32)
    part = iota((PEERS, ROWS), 0)
    aux = jnp.where(
        part == 0,
        lax.shift_right_logical(local, 5),
        jnp.where(part == 1, jnp.bitwise_and(local, 31), 1),
    )
    return slot, aux.astype(F32).astype(BF)


def pack_kernel(tgt_ref, pts_ref, cot_ref, spts_ref, scot_ref, place_ref, slot_ref):
    slot, aux = slot_rows(tgt_ref[...])
    slot_ref[...] = slot
    for peer in range(PEERS):
        mine = one_hot(iota((ROOM, ROWS), 0) + peer * ROOM == slot)
        spts_ref[peer] = dot(mine, pts_ref[...]).astype(BF)
        scot_ref[peer] = dot(mine, cot_ref[...]).astype(BF)
        found = dot_nt(aux, mine)
        place = jnp.where(
            found[2:3] > 0.5, found[0:1] * 32.0 + found[1:2], float(ROWS)
        ).astype(jnp.int32)
        place_ref[peer] = jnp.broadcast_to(place, (8, ROOM))


def unpack_kernel(slot_ref, bres_ref, bgrad_ref, res_ref, grad_ref):
    back_r = bres_ref[...].reshape(SLOTS, C)
    back_g = bgrad_ref[...].reshape(SLOTS, C)
    for block in range(ROWS // 128):
        col = column_of(slot_ref[:, block * 128 : (block + 1) * 128].astype(F32))
        mine = one_hot(iota((128, SLOTS), 1) == col.astype(jnp.int32))
        rows = slice(block * 128, (block + 1) * 128)
        res_ref[rows, :] = dot(mine, back_r).astype(BF)
        grad_ref[rows, :] = dot(mine, back_g).astype(BF)


def place_rows(place_ref, recv_ref, out_ref):
    recv = recv_ref[...].reshape(SLOTS, C)

    for block in range(NB):
        pieces = [
            one_hot(iota((BLK, ROOM), 0) + block * BLK == place_ref[peer, 0:1, :])
            for peer in range(PEERS)
        ]
        out_ref[block * BLK : (block + 1) * BLK, :] = dot(
            jnp.concatenate(pieces, axis=1), recv
        ).astype(BF)


def back_rows(place_ref, rows_ref, out_ref):
    rows = rows_ref[...]
    for peer in range(PEERS):
        col = column_of(place_ref[peer, 0:1, :].astype(F32)).astype(jnp.int32)
        out_ref[peer] = dot(one_hot(iota((ROOM, ROWS), 1) == col), rows).astype(BF)


def first_part(x_ref, w_ref, s):
    normed, _ = normalize(x_ref[...].astype(F32))
    first = normed.astype(BF)
    s.first_t[...] = transpose_bf(first)
    qs = (dot(first, w_ref[:, 0:C]).astype(BF).astype(F32) * 0.25).astype(BF)
    k = dot(first, w_ref[:, C : 2 * C]).astype(BF)
    v = dot(first, w_ref[:, 2 * C : 3 * C]).astype(BF)
    s.q[...] = qs
    s.k[...] = k
    s.v[...] = v
    s.qt[...] = transpose_bf(qs)
    s.kt[...] = (k.astype(F32).T * 0.25).astype(BF)
    v_t = transpose_bf(v)
    s.vt[:, 0:DH, :] = v_t.reshape(HEADS, DH, ROWS)
    s.vt[:, DH : 2 * DH, :] = jnp.ones((HEADS, DH, ROWS), BF)
    s.zq[...] = jnp.zeros((C, ROWS), BF)


def only_head(h, zeroed_ref, rows):
    at = pl.multiple_of(h * DH, DH)
    zeroed_ref[pl.ds(pl.multiple_of(jnp.maximum(h - 1, 0) * DH, DH), DH), :] = jnp.zeros(
        (DH, ROWS), BF
    )
    zeroed_ref[pl.ds(at, DH), :] = rows
    return at


def attend(s):
    @pl.loop(0, HEADS)
    def _(h):
        at = only_head(h, s.zq, s.qt[pl.ds(pl.multiple_of(h * DH, DH), DH), :])
        values = s.vt[h]
        for block in range(NB):
            cols = slice(block * BLK, (block + 1) * BLK)
            scores = dot(s.k[...], s.zq[:, cols])
            raised = jnp.exp(scores - jnp.max(scores, axis=0, keepdims=True)).astype(BF)
            s.p[h, :, cols] = raised
            out = dot(values, raised)
            inverse = 1.0 / out[DH : DH + 1]
            s.ot[pl.ds(at, DH), cols] = (out[0:DH] * inverse).astype(BF)
            s.inv[pl.ds(h, 1), cols] = inverse


def feed_forward(s, x_ref, cot_ref, w_out, w_up, w_down, res_ref):
    @pl.loop(0, NB)
    def _(block):
        rows = pl.ds(pl.multiple_of(block * BLK, BLK), BLK)
        features = x_ref[rows, :].astype(F32)
        tile_grad = cot_ref[rows, :]
        hidden = features + dot(s.att[rows, :], w_out[...])
        normed, inverse = normalize(hidden)
        second = normed.astype(BF)
        s.second[rows, :] = second
        expanded = dot(second, w_up[...])
        activated, slopes = gelu_pair(expanded)
        activated = activated.astype(BF)
        s.act[rows, :] = activated
        res_ref[rows, :] = (hidden + dot(activated, w_down[...])).astype(BF)
        gexp = (dot_nt(tile_grad, w_down[...]) * slopes).astype(BF)
        s.gexp[rows, :] = gexp
        grad_hidden = tile_grad.astype(F32) + norm_back(normed, inverse, dot_nt(gexp, w_up[...]))
        s.gh[rows, :] = grad_hidden
        hrows = grad_hidden.astype(BF)
        s.hrows[rows, :] = hrows
        s.datt[rows, :] = dot_nt(hrows, w_out[...]).astype(BF)


def ff_grads(s, cot_ref, factor, g_out, g_up, g_down):
    g_out[...] = dot(s.ot[...], s.hrows[...]) * factor
    g_up[...] = dot(transpose_bf(s.second[...]), s.gexp[...]) * factor
    g_down[...] = dot(transpose_bf(cot_ref[...]), s.act[...]).T * factor


def attend_back(s):
    dot_t = s.datt[...].astype(F32).T
    inverse = s.inv[...].reshape(HEADS, 1, ROWS)
    don_t = (dot_t.reshape(HEADS, DH, ROWS) * inverse).astype(BF)
    inner = jnp.sum(
        don_t.astype(F32) * s.ot[...].astype(F32).reshape(HEADS, DH, ROWS), axis=1, keepdims=True
    )
    s.inner[...] = inner.reshape(HEADS, ROWS)
    s.dont[...] = don_t.reshape(C, ROWS)
    s.don[...] = transpose_bf(s.dont[...])
    s.zq[...] = jnp.zeros((C, ROWS), BF)

    @pl.loop(0, HEADS)
    def _(h):
        at = only_head(h, s.zq, s.dont[pl.ds(pl.multiple_of(h * DH, DH), DH), :])
        keys = s.kt[pl.ds(at, DH), :]
        for block in range(NB):
            cols = slice(block * BLK, (block + 1) * BLK)
            dp = dot(s.v[...], s.zq[:, cols])
            ds = (s.p[h, :, cols].astype(F32) * (dp - s.inner[pl.ds(h, 1), cols])).astype(BF)
            s.ds[:, cols] = ds
            s.dqt[pl.ds(at, DH), cols] = dot(keys, ds).astype(BF)
        mine = lax.shift_right_logical(iota((ROWS, C), 1), 4) == h
        s.dv[...] = jnp.where(mine, dot(s.p[h], s.don[...]), s.dv[...].astype(F32)).astype(BF)
        s.dk[...] = jnp.where(mine, dot(s.ds[...], s.q[...]), s.dk[...].astype(F32)).astype(BF)


def last_part(s, x_ref, w_ref, factor, g_qkv, grad_ref):
    dq = transpose_bf(s.dqt[...])
    dk = s.dk[...]
    dv = s.dv[...]
    g_first = dot_nt(dq, w_ref[:, 0:C]) + dot_nt(dk, w_ref[:, C : 2 * C])
    g_first = (g_first + dot_nt(dv, w_ref[:, 2 * C : 3 * C])).astype(BF).astype(F32)
    g_qkv[:, 0:C] = dot(s.first_t[...], dq) * factor
    g_qkv[:, C : 2 * C] = dot(s.first_t[...], dk) * factor
    g_qkv[:, 2 * C : 3 * C] = dot(s.first_t[...], dv) * factor
    normed, inverse = normalize(x_ref[...].astype(F32))
    grad_ref[...] = (s.gh[...] + norm_back(normed, inverse, g_first)).astype(BF)


class Scratch:
    shapes = dict(
        x=((ROWS, C), BF), cot=((ROWS, C), BF), first_t=((C, ROWS), BF),
        q=((ROWS, C), BF), k=((ROWS, C), BF), v=((ROWS, C), BF),
        qt=((C, ROWS), BF), kt=((C, ROWS), BF), vt=((HEADS, 2 * DH, ROWS), BF),
        zq=((C, ROWS), BF), p=((HEADS, ROWS, ROWS), BF), ot=((C, ROWS), BF),
        inv=((HEADS, ROWS), F32), att=((ROWS, C), BF), second=((ROWS, C), BF),
        act=((ROWS, FF), BF), gexp=((ROWS, FF), BF), gh=((ROWS, C), F32),
        hrows=((ROWS, C), BF), datt=((ROWS, C), BF), inner=((HEADS, ROWS), F32),
        dont=((C, ROWS), BF), don=((ROWS, C), BF),
        dqt=((C, ROWS), BF), dv=((ROWS, C), BF), dk=((ROWS, C), BF),
    )

    def __init__(self, refs):
        for name, ref in zip(self.shapes, refs):
            setattr(self, name, ref)
        self.ds = self.act
        self.out = self.att

    @classmethod
    def specs(cls):
        return [pltpu.VMEM(*v) for v in cls.shapes.values()]


def core_kernel(
    factor, rpts, rcot, place, w_qkv, w_out, w_up, w_down,
    bres, bgrad, g_qkv, g_out, g_up, g_down, *scratch,
):
    s = Scratch(scratch)
    place_rows(place, rpts, s.x)
    first_part(s.x, w_qkv, s)
    attend(s)
    place_rows(place, rcot, s.cot)
    s.att[...] = transpose_bf(s.ot[...])
    feed_forward(s, s.x, s.cot, w_out, w_up, w_down, s.out)
    back_rows(place, s.out, bres)
    ff_grads(s, s.cot, factor, g_out, g_up, g_down)
    attend_back(s)
    last_part(s, s.x, w_qkv, factor, g_qkv, s.out)
    back_rows(place, s.out, bgrad)


VM = pl.BlockSpec(memory_space=pltpu.VMEM)
LIMIT = 65000 * 1024


def call(kernel, ins, outs, scratch=()):
    return pl.pallas_call(
        kernel,
        out_shape=[jax.ShapeDtypeStruct(*o) for o in outs],
        in_specs=[VM] * len(ins),
        out_specs=[VM] * len(outs),
        scratch_shapes=list(scratch),
        compiler_params=pltpu.CompilerParams(vmem_limit_bytes=LIMIT),
    )(*ins)


SENT = ((PEERS, ROOM, C), BF)
GRADS = [((C, 3 * C), F32), ((C, C), F32), ((C, FF), F32), ((FF, C), F32)]


def exchange(values):
    return lax.all_to_all(values, "seq", split_axis=0, concat_axis=0, tiled=True)


def core(factor, rpts, rcot, place, *weights):
    return call(
        lambda *refs: core_kernel(factor, *refs),
        (rpts, rcot, place, *weights),
        [SENT, SENT, *GRADS],
        Scratch.specs(),
    )


def body(points, targets, cotangent, w_qkv, w_out, w_up, w_down):
    row_count = points.shape[1]
    factor = 1.0 / math.sqrt(
        points.shape[0] * lax.axis_size("dp") * lax.axis_size("seq") * row_count
    )
    spts, scot, place, slot = call(
        pack_kernel,
        (targets, points[0], cotangent[0]),
        [SENT, SENT, ((PEERS, 8, ROOM), jnp.int32), ((1, ROWS), jnp.int32)],
    )
    place = exchange(place)
    rpts = exchange(spts)
    rcot = exchange(scot)
    bres, bgrad, *grads = core(factor, rpts, rcot, place, w_qkv, w_out, w_up, w_down)
    result, grad_points = call(
        unpack_kernel,
        (slot, exchange(bres), exchange(bgrad)),
        [((ROWS, C), BF), ((ROWS, C), BF)],
    )
    summed = lax.psum(tuple(grads), ("seq", "dp"))
    return (result[None], grad_points[None], *summed)


def solution(mesh):
    return jax.shard_map(
        body,
        mesh=mesh,
        in_specs=(P("dp", "seq", None), P("dp", "seq"), P("dp", "seq", None), P(), P(), P(), P()),
        out_specs=(P("dp", "seq", None), P("dp", "seq", None), P(), P(), P(), P()),
        check_vma=False,
    )
```

```python
import math

import jax
import jax.numpy as jnp
from jax import lax
from jax.experimental import pallas as pl
from jax.experimental.pallas import tpu as pltpu
from jax.sharding import PartitionSpec as P

BF = jnp.bfloat16
F32 = jnp.float32
C = 256
HEADS = 16
DH = 16
FF = 1024
ROWS = 1024
PEERS = 16
ROOM = 128
SLOTS = PEERS * ROOM
BLK = 256
NB = ROWS // BLK
HALF = 128
EPS = 1e-05
GELU_A = 0.7978845608028654
GELU_B = 0.044715


def dot(left, right):
    return lax.dot_general(left, right, (((1,), (0,)), ((), ())), preferred_element_type=F32)


def dot_nt(left, right):
    return lax.dot_general(left, right, (((1,), (1,)), ((), ())), preferred_element_type=F32)


def iota(shape, axis):
    return lax.broadcasted_iota(jnp.int32, shape, axis)


def one_hot(cond):
    return jnp.where(cond, 1.0, 0.0).astype(BF)


def transpose_bf(values):
    return values.astype(F32).T.astype(BF)


def normalize(values):
    center = jnp.mean(values, axis=-1, keepdims=True)
    shifted = values - center
    inverse_std = lax.rsqrt(jnp.mean(shifted * shifted, axis=-1, keepdims=True) + EPS)
    return shifted * inverse_std, inverse_std


def norm_back(normed, inverse_std, upstream):
    return inverse_std * (
        upstream
        - jnp.mean(upstream, axis=-1, keepdims=True)
        - normed * jnp.mean(upstream * normed, axis=-1, keepdims=True)
    )


def gelu_pair(inputs):
    square = inputs * inputs
    tangent = jnp.tanh(GELU_A * (inputs + GELU_B * square * inputs))
    half = 0.5 * (1.0 + tangent)
    slopes = half + 0.5 * inputs * (1.0 - tangent * tangent) * GELU_A * (
        1.0 + 3.0 * GELU_B * square
    )
    return inputs * half, slopes


def column_of(row):
    return jnp.broadcast_to(row, (128, 128)).T[:, 0:1]


def slot_rows(targets, me):
    owner = lax.shift_right_logical(targets, 10)
    local = jnp.bitwise_and(targets, ROWS - 1)
    marks = iota((PEERS, ROWS), 0) == owner
    before = one_hot(iota((ROWS, ROWS), 0) < iota((ROWS, ROWS), 1))
    counts = dot(one_hot(marks), before)
    rank = jnp.sum(jnp.where(marks, counts, 0.0), axis=0, keepdims=True)
    slot = jnp.bitwise_and(owner - me, PEERS - 1) * ROOM + rank.astype(jnp.int32)
    part = iota((PEERS, ROWS), 0)
    aux = jnp.where(
        part == 0,
        lax.shift_right_logical(local, 5),
        jnp.where(part == 1, jnp.bitwise_and(local, 31), 1),
    )
    return slot, aux.astype(F32).astype(BF)


def home_rows(s, back, out_ref):
    rows = back[...].reshape(SLOTS, C)
    for block in range(ROWS // 128):
        at = slice(block * 128, (block + 1) * 128)
        col = column_of(s.slot[:, at].astype(F32)).astype(jnp.int32)
        out_ref[at, :] = dot(one_hot(iota((128, SLOTS), 1) == col), rows).astype(BF)


def place_rows(s, recv_ref, out_ref):
    recv = recv_ref[...].reshape(SLOTS, C)
    for block in range(NB):
        pieces = [
            one_hot(iota((BLK, ROOM), 0) + block * BLK == s.place[peer, 0:1, :])
            for peer in range(PEERS)
        ]
        out_ref[block * BLK : (block + 1) * BLK, :] = dot(
            jnp.concatenate(pieces, axis=1), recv
        ).astype(BF)


def first_part(s, w_ref):
    normed, _ = normalize(s.x[...].astype(F32))
    first = normed.astype(BF)
    s.first_t[...] = transpose_bf(first)
    qs = (dot(first, w_ref[:, 0:C]).astype(BF).astype(F32) * 0.25).astype(BF)
    k = dot(first, w_ref[:, C : 2 * C]).astype(BF)
    v = dot(first, w_ref[:, 2 * C : 3 * C]).astype(BF)
    s.q[...] = qs
    s.k[...] = k
    s.v[...] = v
    s.qt[...] = transpose_bf(qs)
    s.kt[...] = transpose_bf(k)
    for half in range(2):
        s.va[half, :, 0:HALF] = v[:, half * HALF : (half + 1) * HALF]
        s.va[half, :, HALF:C] = jnp.ones((ROWS, HALF), BF)
    s.za[...] = jnp.zeros((C, ROWS), BF)


def head_rows(h):
    return pl.ds(pl.multiple_of(h * DH, DH), DH)


def only_head(h, zeroed_ref, rows):
    zeroed_ref[head_rows(jnp.maximum(h - 1, 0)), :] = jnp.zeros((DH, ROWS), BF)
    zeroed_ref[head_rows(h), :] = rows


def attend(s):
    @pl.loop(0, HEADS)
    def _(h):
        half = h // 8
        only_head(h, s.za, s.kt[head_rows(h), :])
        lane = iota((HALF, HALF), 1)
        for block in range(ROWS // HALF):
            rows = slice(block * HALF, (block + 1) * HALF)
            scores = dot(s.q[rows, :], s.za[...])
            top = jnp.max(scores, axis=1, keepdims=True)
            out = dot(jnp.exp(scores - top).astype(BF), s.va[half])
            total = out[:, HALF : HALF + 1]
            s.heads[half, rows, :] = jnp.where(
                lax.shift_right_logical(lane, 4) == h - 8 * half,
                out[:, 0:HALF] * (1.0 / total),
                s.heads[half, rows, :],
            )
            s.lse[rows, :] = jnp.where(lane == h, top + jnp.log(total), s.lse[rows, :])


def feed_forward(s, w_out, w_up, w_down):
    @pl.loop(0, NB)
    def _(block):
        rows = pl.ds(pl.multiple_of(block * BLK, BLK), BLK)
        features = s.x[rows, :].astype(F32)
        tile_grad = s.cot[rows, :]
        hidden = features + dot(s.att[rows, :], w_out[...])
        normed, inverse = normalize(hidden)
        second = normed.astype(BF)
        s.second[rows, :] = second
        expanded = dot(second, w_up[...])
        activated, slopes = gelu_pair(expanded)
        activated = activated.astype(BF)
        s.act[rows, :] = activated
        s.out[rows, :] = (hidden + dot(activated, w_down[...])).astype(BF)
        gexp = (dot_nt(tile_grad, w_down[...]) * slopes).astype(BF)
        s.gexp[rows, :] = gexp
        grad_hidden = tile_grad.astype(F32) + norm_back(normed, inverse, dot_nt(gexp, w_up[...]))
        s.gh[rows, :] = grad_hidden
        hrows = grad_hidden.astype(BF)
        s.hrows[rows, :] = hrows
        s.datt[rows, :] = dot_nt(hrows, w_out[...]).astype(BF)


def attend_back(s, steps):
    dot_t = s.datt[...].astype(F32).T
    s.dot_t[...] = dot_t.astype(BF)
    inner = (dot_t * s.ot[...].astype(F32)).reshape(HEADS, DH, ROWS)
    s.inner[...] = jnp.sum(inner, axis=1, keepdims=True).reshape(HEADS, ROWS)
    s.lse_t[...] = s.lse[...].T[0:HEADS]
    s.za[...] = jnp.zeros((C, ROWS), BF)
    s.zb[...] = jnp.zeros((C, ROWS), BF)

    @pl.loop(0, HEADS)
    def _(h):
        for when, step in steps.items():
            pl.when(h == when)(step)
        only_head(h, s.za, s.qt[head_rows(h), :])
        only_head(h, s.zb, s.dot_t[head_rows(h), :])
        keys = s.kt[head_rows(h), :]
        for block in range(NB):
            cols = slice(block * BLK, (block + 1) * BLK)
            probs = jnp.exp(dot(s.k[...], s.za[:, cols]) - s.lse_t[pl.ds(h, 1), cols])
            dp = dot(s.v[...], s.zb[:, cols])
            ds = (probs * (dp - s.inner[pl.ds(h, 1), cols])).astype(BF)
            s.p[:, cols] = probs.astype(BF)
            s.ds[:, cols] = ds
            s.dqt[head_rows(h), cols] = (dot(keys, ds) * 0.25).astype(BF)
        mine = lax.shift_right_logical(iota((ROWS, C), 1), 4) == h
        s.dv[...] = jnp.where(mine, dot(s.p[...], s.datt[...]), s.dv[...])
        s.dk[...] = jnp.where(mine, dot(s.ds[...], s.q[...]), s.dk[...])


class Copies:
    def __init__(self, axis, size, me, sign, source, target, send, recv):
        self.parts = {}
        for d in range(1, size):
            peer = lax.rem(me + (d if sign > 0 else size - d), size)
            self.parts[d] = pltpu.make_async_remote_copy(
                src_ref=source(d, peer),
                dst_ref=target(d),
                send_sem=send.at[d],
                recv_sem=recv.at[d],
                device_id={axis: peer},
                device_id_type=pl.DeviceIdType.MESH,
            )

    def start(self, d=None):
        for key, part in self.parts.items():
            if d is None or key == d:
                part.start()

    def arrived(self):
        for part in self.parts.values():
            part.wait_recv()

    def sent(self):
        for part in self.parts.values():
            part.wait_send()


class Reduction:
    def __init__(self, s, name, seq, zed, n_dp, split):
        self.seq, self.zed, self.n_dp, self.split = seq, zed, n_dp, split
        self.own, self.got, self.cut, self.cut_got, self.fin, self.all = (
            getattr(s, name + part) for part in ("own", "got", "cut", "cutgot", "fin", "all")
        )
        sems = [(getattr(s, f"{name}send{i}"), getattr(s, f"{name}recv{i}")) for i in range(4)]
        self.first = lambda: Copies(
            "dp", n_dp, zed, 1, lambda d, p: self.own.at[p], lambda d: self.got.at[d], *sems[0]
        )
        self.second = lambda: Copies(
            "seq", PEERS, seq, 1, lambda d, p: self.cut.at[p], lambda d: self.cut_got.at[d], *sems[1]
        )
        self.third = lambda: Copies(
            "seq", PEERS, seq, 1, lambda d, p: self.fin.at[seq], lambda d: self.fin.at[seq], *sems[2]
        )
        self.fourth = lambda: Copies(
            "dp", n_dp, zed, 1, lambda d, p: self.all.at[zed], lambda d: self.all.at[zed], *sems[3]
        )

    def spots(self):
        rows, cols = self.cut.shape[1:]
        for piece in range(PEERS):
            up, along = (piece // 8, piece % 8) if self.split else (0, piece)
            yield piece, slice(up * rows, (up + 1) * rows), slice(along * cols, (along + 1) * cols)

    def step0(self):
        self.first().start()

    def step1(self):
        self.first().arrived()
        for piece, rows, cols in self.spots():
            total = self.own[self.zed, rows, cols].astype(F32)
            for d in range(1, self.n_dp):
                total = total + self.got[d, rows, cols].astype(F32)
            self.cut[piece] = total
        self.second().start()

    def step2(self):
        self.second().arrived()
        total = self.cut[self.seq]
        for d in range(1, PEERS):
            total = total + self.cut_got[d]
        self.fin[self.seq] = total.astype(BF)
        self.third().start()

    def step3(self):
        self.third().arrived()
        for piece, rows, cols in self.spots():
            self.all[self.zed, rows, cols] = self.fin[piece]
        self.fourth().start()

    def step4(self, out_ref):
        self.fourth().arrived()
        out_ref[...] = self.all[...].reshape(out_ref.shape)
        for copies in (self.first, self.second, self.third, self.fourth):
            copies().sent()


def scratch_of(n_dp):
    rows = C // n_dp
    room, tall, flat, sent = (PEERS, ROOM, C), (ROWS, C), (C, ROWS), pltpu.SemaphoreType.DMA
    names = {}
    for name in ("x", "cot", "q", "k", "v", "att", "second", "hrows", "datt", "out"):
        names[name] = pltpu.VMEM(tall, BF)
    for name in ("gh", "dv", "dk"):
        names[name] = pltpu.VMEM(tall, F32)
    for name in ("first_t", "qt", "kt", "za", "zb", "ot", "dot_t", "dqt"):
        names[name] = pltpu.VMEM(flat, BF)
    for name in ("act", "gexp", "p", "ds"):
        names[name] = pltpu.VMEM((ROWS, FF), BF)
    for name in ("inner", "lse_t"):
        names[name] = pltpu.VMEM((HEADS, ROWS), F32)
    names["lse"] = pltpu.VMEM((ROWS, HALF), F32)
    names["va"] = pltpu.VMEM((2, ROWS, C), BF)
    names["heads"] = pltpu.VMEM((2, ROWS, HALF), F32)
    names["slot"] = pltpu.VMEM((1, ROWS), jnp.int32)
    for name in ("place", "splace"):
        names[name] = pltpu.VMEM((PEERS, 8, ROOM), jnp.int32)
    for name in ("spts", "scot", "sres", "sgrad", "rpts", "rcot", "rres", "rgrad"):
        names[name] = pltpu.VMEM(room, BF)
    for name in ("place", "pts", "cot", "res", "grad"):
        names["send" + name] = sent((PEERS,))
        names["recv" + name] = sent((PEERS,))
    for name, wide, piece in (("a", 2 * FF, (rows, HALF)), ("b", 4 * C, (rows // 2, HALF))):
        for part in ("own", "got", "all"):
            names[name + part] = pltpu.VMEM((n_dp, rows, wide), BF)
        for part in ("cut", "cutgot"):
            names[name + part] = pltpu.VMEM((PEERS, *piece), F32)
        names[name + "fin"] = pltpu.VMEM((PEERS, *piece), BF)
        for step in range(4):
            names[f"{name}send{step}"] = sent((PEERS,))
            names[f"{name}recv{step}"] = sent((PEERS,))
    return names


class Scratch:
    def __init__(self, names, refs):
        for name, ref in zip(names, refs):
            setattr(self, name, ref)


def kernel(
    n_dp, names, tgt, pts, cot, w_qkv, w_out, w_up, w_down,
    res_out, grad_out, a_out, b_out, *refs,
):
    s = Scratch(names, refs)
    seq, zed = lax.axis_index("seq"), lax.axis_index("dp")
    barrier = pltpu.get_barrier_semaphore()
    for axis, size, me in (("seq", PEERS, seq), ("dp", n_dp, zed)):
        for d in range(1, size):
            pl.semaphore_signal(
                barrier,
                inc=1,
                device_id={axis: lax.rem(me + d, size)},
                device_id_type=pl.DeviceIdType.MESH,
            )

    def exchange(name, sign, source, target):
        return Copies(
            "seq", PEERS, seq, sign, lambda d, p: source.at[d], lambda d: target.at[d],
            getattr(s, "send" + name), getattr(s, "recv" + name),
        )

    go_place = exchange("place", 1, s.splace, s.place)
    go_pts = exchange("pts", 1, s.spts, s.rpts)
    go_cot = exchange("cot", 1, s.scot, s.rcot)
    go_res = exchange("res", -1, s.sres, s.rres)
    go_grad = exchange("grad", -1, s.sgrad, s.rgrad)

    slot, aux = slot_rows(tgt[...], seq)
    s.slot[...] = slot
    pl.semaphore_wait(barrier, PEERS - 1 + n_dp - 1)
    for d in [*range(1, PEERS), 0]:
        mine = one_hot(iota((ROOM, ROWS), 0) + d * ROOM == slot)
        found = dot_nt(aux, mine)
        place = jnp.where(
            found[2:3] > 0.5, found[0:1] * 32.0 + found[1:2], float(ROWS)
        ).astype(jnp.int32)
        place = jnp.broadcast_to(place, (8, ROOM))
        block = dot(mine, pts[...]).astype(BF)
        if d:
            s.splace[d] = place
            s.spts[d] = block
            go_place.start(d)
            go_pts.start(d)
        else:
            s.place[0] = place
            s.rpts[0] = block
    for d in [*range(1, PEERS), 0]:
        mine = one_hot(iota((ROOM, ROWS), 0) + d * ROOM == slot)
        block = dot(mine, cot[...]).astype(BF)
        if d:
            s.scot[d] = block
            go_cot.start(d)
        else:
            s.rcot[0] = block

    def send_back(go, rows_ref, mine_ref, theirs_ref):
        rows = rows_ref[...]
        for d in [*range(1, PEERS), 0]:
            col = column_of(s.place[d, 0:1, :].astype(F32)).astype(jnp.int32)
            block = dot(one_hot(iota((ROOM, ROWS), 1) == col), rows).astype(BF)
            if d:
                theirs_ref[d] = block
                go.start(d)
            else:
                mine_ref[0] = block

    go_place.arrived()
    go_pts.arrived()
    place_rows(s, s.rpts, s.x)
    first_part(s, w_qkv)
    attend(s)
    for half in range(2):
        s.att[:, half * HALF : (half + 1) * HALF] = s.heads[half].astype(BF)
    s.ot[...] = transpose_bf(s.att[...])
    go_cot.arrived()
    place_rows(s, s.rcot, s.cot)
    feed_forward(s, w_out, w_up, w_down)
    send_back(go_res, s.out, s.rres, s.sres)

    wide = Reduction(s, "a", seq, zed, n_dp, False)
    last = Reduction(s, "b", seq, zed, n_dp, True)

    def put(ref, values, at):
        ref[:, :, at : at + values.shape[1]] = values.astype(BF).reshape(
            n_dp, C // n_dp, values.shape[1]
        )

    put(s.aown, dot(transpose_bf(s.second[...]), s.gexp[...]), 0)
    put(s.aown, dot(transpose_bf(s.cot[...]), s.act[...]), FF)
    wide.step0()
    put(s.bown, dot(s.ot[...], s.hrows[...]), 3 * C)
    attend_back(s, {5: wide.step1, 8: wide.step2, 10: wide.step3})

    dq = transpose_bf(s.dqt[...])
    dk = s.dk[...].astype(BF)
    dv = s.dv[...].astype(BF)
    put(s.bown, dot(s.first_t[...], dq), 0)
    put(s.bown, dot(s.first_t[...], dk), C)
    put(s.bown, dot(s.first_t[...], dv), 2 * C)
    last.step0()
    g_first = dot_nt(dq, w_qkv[:, 0:C]) + dot_nt(dk, w_qkv[:, C : 2 * C])
    g_first = (g_first + dot_nt(dv, w_qkv[:, 2 * C : 3 * C])).astype(BF).astype(F32)
    normed, inverse = normalize(s.x[...].astype(F32))
    s.out[...] = (s.gh[...] + norm_back(normed, inverse, g_first)).astype(BF)
    send_back(go_grad, s.out, s.rgrad, s.sgrad)
    last.step1()
    go_res.arrived()
    home_rows(s, s.rres, res_out)
    last.step2()
    wide.step4(a_out)
    last.step3()
    go_grad.arrived()
    home_rows(s, s.rgrad, grad_out)
    last.step4(b_out)
    for go in (go_place, go_pts, go_cot, go_res, go_grad):
        go.sent()


def body(points, targets, cotangent, w_qkv, w_out, w_up, w_down):
    n_dp = lax.axis_size("dp")
    factor = 1.0 / math.sqrt(points.shape[0] * n_dp * lax.axis_size("seq") * points.shape[1])
    names = scratch_of(n_dp)
    vmem = pl.BlockSpec(memory_space=pltpu.VMEM)
    result, grad_points, wide, last = pl.pallas_call(
        lambda *refs: kernel(n_dp, list(names), *refs),
        out_shape=[
            jax.ShapeDtypeStruct((ROWS, C), BF),
            jax.ShapeDtypeStruct((ROWS, C), BF),
            jax.ShapeDtypeStruct((C, 2 * FF), BF),
            jax.ShapeDtypeStruct((C, 4 * C), BF),
        ],
        in_specs=[vmem] * 7,
        out_specs=[vmem] * 4,
        scratch_shapes=list(names.values()),
        compiler_params=pltpu.CompilerParams(
            vmem_limit_bytes=60 * 1024 * 1024, collective_id=0, has_side_effects=True
        ),
    )(targets, points[0], cotangent[0], w_qkv, w_out, w_up, w_down)
    wide = wide.astype(F32) * factor
    last = last.astype(F32) * factor
    return (
        result[None],
        grad_points[None],
        last[:, 0 : 3 * C],
        last[:, 3 * C :],
        wide[:, 0:FF],
        wide[:, FF:].T,
    )


def solution(mesh):
    return jax.shard_map(
        body,
        mesh=mesh,
        in_specs=(P("dp", "seq", None), P("dp", "seq"), P("dp", "seq", None), P(), P(), P(), P()),
        out_specs=(P("dp", "seq", None), P("dp", "seq", None), P(), P(), P(), P()),
        check_vma=False,
    )
```

```python
import math

import jax
import jax.numpy as jnp
from jax import lax
from jax.experimental import pallas as pl
from jax.experimental.pallas import tpu as pltpu
from jax.sharding import PartitionSpec as P

BF = jnp.bfloat16
F32 = jnp.float32
C = 256
HEADS = 16
DH = 16
FF = 1024
ROWS = 1024
PEERS = 16
ROOM = 128
SLOTS = PEERS * ROOM
BLK = 256
NB = ROWS // BLK
HALF = 128
EPS = 1e-05
GELU_A = 0.7978845608028654
GELU_B = 0.044715


def dot(left, right):
    return lax.dot_general(left, right, (((1,), (0,)), ((), ())), preferred_element_type=F32)


def dot_nt(left, right):
    return lax.dot_general(left, right, (((1,), (1,)), ((), ())), preferred_element_type=F32)


def iota(shape, axis):
    return lax.broadcasted_iota(jnp.int32, shape, axis)


def one_hot(cond):
    return jnp.where(cond, 1.0, 0.0).astype(BF)


def transpose_bf(values):
    return values.astype(F32).T.astype(BF)


def normalize(values):
    center = jnp.mean(values, axis=-1, keepdims=True)
    shifted = values - center
    inverse_std = lax.rsqrt(jnp.mean(shifted * shifted, axis=-1, keepdims=True) + EPS)
    return shifted * inverse_std, inverse_std


def norm_back(normed, inverse_std, upstream):
    return inverse_std * (
        upstream
        - jnp.mean(upstream, axis=-1, keepdims=True)
        - normed * jnp.mean(upstream * normed, axis=-1, keepdims=True)
    )


def gelu_pair(inputs):
    square = inputs * inputs
    tangent = jnp.tanh(GELU_A * (inputs + GELU_B * square * inputs))
    half = 0.5 * (1.0 + tangent)
    slopes = half + 0.5 * inputs * (1.0 - tangent * tangent) * GELU_A * (
        1.0 + 3.0 * GELU_B * square
    )
    return inputs * half, slopes


def column_of(row):
    return jnp.broadcast_to(row, (128, 128)).T[:, 0:1]


def slot_rows(targets, me):
    owner = lax.shift_right_logical(targets, 10)
    local = jnp.bitwise_and(targets, ROWS - 1)
    marks = iota((PEERS, ROWS), 0) == owner
    before = one_hot(iota((ROWS, ROWS), 0) < iota((ROWS, ROWS), 1))
    counts = dot(one_hot(marks), before)
    rank = jnp.sum(jnp.where(marks, counts, 0.0), axis=0, keepdims=True)
    slot = jnp.bitwise_and(owner - me, PEERS - 1) * ROOM + rank.astype(jnp.int32)
    part = iota((PEERS, ROWS), 0)
    aux = jnp.where(
        part == 0,
        lax.shift_right_logical(local, 5),
        jnp.where(part == 1, jnp.bitwise_and(local, 31), 1),
    )
    return slot, aux.astype(F32).astype(BF)


def home_rows(s, back, out_ref):
    rows = back[...].reshape(SLOTS, C)
    for block in range(ROWS // 128):
        at = slice(block * 128, (block + 1) * 128)
        col = column_of(s.slot[:, at].astype(F32)).astype(jnp.int32)
        out_ref[at, :] = dot(one_hot(iota((128, SLOTS), 1) == col), rows).astype(BF)


def place_rows(s, recv_ref, out_ref):
    recv = recv_ref[...].reshape(SLOTS, C)
    for block in range(NB):
        pieces = [
            one_hot(iota((BLK, ROOM), 0) + block * BLK == s.place[peer, 0:1, :])
            for peer in range(PEERS)
        ]
        out_ref[block * BLK : (block + 1) * BLK, :] = dot(
            jnp.concatenate(pieces, axis=1), recv
        ).astype(BF)


def first_part(s, w_ref):
    normed, _ = normalize(s.x[...].astype(F32))
    first = normed.astype(BF)
    s.first_t[...] = transpose_bf(first)
    qs = (dot(first, w_ref[:, 0:C]).astype(BF).astype(F32) * 0.25).astype(BF)
    k = dot(first, w_ref[:, C : 2 * C]).astype(BF)
    v = dot(first, w_ref[:, 2 * C : 3 * C]).astype(BF)
    s.q[...] = qs
    s.k[...] = k
    s.v[...] = v
    s.qt[...] = transpose_bf(qs)
    s.kt[...] = transpose_bf(k)
    for half in range(2):
        s.va[half, :, 0:HALF] = v[:, half * HALF : (half + 1) * HALF]
        s.va[half, :, HALF:C] = jnp.ones((ROWS, HALF), BF)
    s.za[...] = jnp.zeros((C, ROWS), BF)


def head_rows(h):
    return pl.ds(pl.multiple_of(h * DH, DH), DH)


def only_head(h, zeroed_ref, rows):
    zeroed_ref[head_rows(jnp.maximum(h - 1, 0)), :] = jnp.zeros((DH, ROWS), BF)
    zeroed_ref[head_rows(h), :] = rows


def attend(s):
    @pl.loop(0, HEADS, unroll=2)
    def _(h):
        half = h // 8
        only_head(h, s.za, s.kt[head_rows(h), :])
        lane = iota((HALF, HALF), 1)
        for block in range(ROWS // HALF):
            rows = slice(block * HALF, (block + 1) * HALF)
            scores = dot(s.q[rows, :], s.za[...])
            top = jnp.max(scores, axis=1, keepdims=True)
            out = dot(jnp.exp(scores - top).astype(BF), s.va[half])
            total = out[:, HALF : HALF + 1]
            s.heads[half, rows, :] = jnp.where(
                lax.shift_right_logical(lane, 4) == h - 8 * half,
                out[:, 0:HALF] * (1.0 / total),
                s.heads[half, rows, :],
            )
            s.lse[rows, :] = jnp.where(lane == h, top + jnp.log(total), s.lse[rows, :])


def feed_forward(s, w_out, w_up, w_down):
    @pl.loop(0, NB)
    def _(block):
        rows = pl.ds(pl.multiple_of(block * BLK, BLK), BLK)
        features = s.x[rows, :].astype(F32)
        tile_grad = s.cot[rows, :]
        hidden = features + dot(s.att[rows, :], w_out[...])
        normed, inverse = normalize(hidden)
        second = normed.astype(BF)
        s.second[rows, :] = second
        expanded = dot(second, w_up[...])
        activated, slopes = gelu_pair(expanded)
        activated = activated.astype(BF)
        s.act[rows, :] = activated
        s.out[rows, :] = (hidden + dot(activated, w_down[...])).astype(BF)
        gexp = (dot_nt(tile_grad, w_down[...]) * slopes).astype(BF)
        s.gexp[rows, :] = gexp
        grad_hidden = tile_grad.astype(F32) + norm_back(normed, inverse, dot_nt(gexp, w_up[...]))
        s.gh[rows, :] = grad_hidden
        hrows = grad_hidden.astype(BF)
        s.hrows[rows, :] = hrows
        s.datt[rows, :] = dot_nt(hrows, w_out[...]).astype(BF)


def prepare_back(s):
    dot_t = s.datt[...].astype(F32).T
    s.dot_t[...] = dot_t.astype(BF)
    inner = (dot_t * s.ot[...].astype(F32)).reshape(HEADS, DH, ROWS)
    s.inner[...] = jnp.sum(inner, axis=1, keepdims=True).reshape(HEADS, ROWS)
    s.lse_t[...] = s.lse[...].T[0:HEADS]
    s.za[...] = jnp.zeros((C, ROWS), BF)
    s.zb[...] = jnp.zeros((C, ROWS), BF)


def attend_back(s, steps):
    @pl.loop(0, HEADS // 2)
    def _(pair):
        for when, step in steps.items():
            pl.when(pair == when)(step)
        for odd in range(2):
            head_back(s, pair * 2 + odd)


def head_back(s, h):
    only_head(h, s.za, s.qt[head_rows(h), :])
    only_head(h, s.zb, s.dot_t[head_rows(h), :])
    keys = s.kt[head_rows(h), :]
    for block in range(NB):
        cols = slice(block * BLK, (block + 1) * BLK)
        probs = jnp.exp(dot(s.k[...], s.za[:, cols]) - s.lse_t[pl.ds(h, 1), cols])
        dp = dot(s.v[...], s.zb[:, cols])
        ds = (probs * (dp - s.inner[pl.ds(h, 1), cols])).astype(BF)
        s.p[:, cols] = probs.astype(BF)
        s.ds[:, cols] = ds
        s.dqt[head_rows(h), cols] = (dot(keys, ds) * 0.25).astype(BF)
    mine = lax.shift_right_logical(iota((ROWS, C), 1), 4) == h
    s.dv[...] = jnp.where(mine, dot(s.p[...], s.datt[...]), s.dv[...])
    s.dk[...] = jnp.where(mine, dot(s.ds[...], s.q[...]), s.dk[...])


class Copies:
    def __init__(self, axis, size, me, sign, source, target, send, recv):
        self.parts = {}
        for d in range(1, size):
            peer = lax.rem(me + (d if sign > 0 else size - d), size)
            self.parts[d] = pltpu.make_async_remote_copy(
                src_ref=source(d, peer),
                dst_ref=target(d),
                send_sem=send.at[d],
                recv_sem=recv.at[d],
                device_id={axis: peer},
                device_id_type=pl.DeviceIdType.MESH,
            )

    def start(self, d=None):
        for key, part in self.parts.items():
            if d is None or key == d:
                part.start()

    def arrived(self):
        for part in self.parts.values():
            part.wait_recv()

    def sent(self):
        for part in self.parts.values():
            part.wait_send()


class Reduction:
    def __init__(self, s, name, seq, zed, n_dp):
        self.seq, self.zed, self.n_dp = seq, zed, n_dp
        self.own, self.got, self.cut, self.cut_got, self.fin, self.all = (
            getattr(s, name + part) for part in ("own", "got", "cut", "cutgot", "fin", "all")
        )
        sems = [(getattr(s, f"{name}send{i}"), getattr(s, f"{name}recv{i}")) for i in range(4)]
        self.first = lambda: Copies(
            "dp", n_dp, zed, 1, lambda d, p: self.own.at[p], lambda d: self.got.at[d], *sems[0]
        )
        self.second = lambda: Copies(
            "seq", PEERS, seq, 1, lambda d, p: self.cut.at[p], lambda d: self.cut_got.at[d], *sems[1]
        )
        self.third = lambda: Copies(
            "seq", PEERS, seq, 1, lambda d, p: self.fin.at[seq], lambda d: self.fin.at[seq], *sems[2]
        )
        self.fourth = lambda: Copies(
            "dp", n_dp, zed, 1, lambda d, p: self.all.at[zed], lambda d: self.all.at[zed], *sems[3]
        )

    def spots(self):
        rows, cols = self.cut.shape[1:]
        across = self.own.shape[2] // cols
        for piece in range(PEERS):
            up, along = piece // across, piece % across
            yield piece, slice(up * rows, (up + 1) * rows), slice(along * cols, (along + 1) * cols)

    def step0(self):
        self.first().start()

    def step1(self):
        self.first().arrived()
        for piece, rows, cols in self.spots():
            total = self.own[self.zed, rows, cols].astype(F32)
            for d in range(1, self.n_dp):
                total = total + self.got[d, rows, cols].astype(F32)
            self.cut[piece] = total
        self.second().start()

    def step2(self):
        self.second().arrived()
        total = self.cut[self.seq]
        for d in range(1, PEERS):
            total = total + self.cut_got[d]
        self.fin[self.seq] = total
        self.third().start()

    def step3(self):
        self.third().arrived()
        across = self.own.shape[2] // self.cut.shape[2]
        bands = [
            jnp.concatenate([self.fin[at + piece] for piece in range(across)], axis=1)
            for at in range(0, PEERS, across)
        ]
        self.all[self.zed] = jnp.concatenate(bands, axis=0).astype(BF)
        self.fourth().start()

    def step4(self, out_ref):
        self.fourth().arrived()
        out_ref[...] = self.all[...].reshape(out_ref.shape)
        for copies in (self.first, self.second, self.third, self.fourth):
            copies().sent()


def scratch_of(n_dp):
    rows = C // n_dp
    room, tall, flat, sent = (PEERS, ROOM, C), (ROWS, C), (C, ROWS), pltpu.SemaphoreType.DMA
    names = {}
    for name in ("x", "cot", "dq", "q", "k", "v", "att", "second", "hrows", "datt", "out"):
        names[name] = pltpu.VMEM(tall, BF)
    for name in ("gh", "dv", "dk"):
        names[name] = pltpu.VMEM(tall, F32)
    for name in ("first_t", "qt", "kt", "za", "zb", "ot", "dot_t", "dqt"):
        names[name] = pltpu.VMEM(flat, BF)
    for name in ("act", "gexp", "p", "ds"):
        names[name] = pltpu.VMEM((ROWS, FF), BF)
    for name in ("inner", "lse_t"):
        names[name] = pltpu.VMEM((HEADS, ROWS), F32)
    names["lse"] = pltpu.VMEM((ROWS, HALF), F32)
    names["va"] = pltpu.VMEM((2, ROWS, C), BF)
    names["heads"] = pltpu.VMEM((2, ROWS, HALF), F32)
    names["slot"] = pltpu.VMEM((1, ROWS), jnp.int32)
    for name in ("place", "splace"):
        names[name] = pltpu.VMEM((PEERS, 8, ROOM), jnp.int32)
    for name in ("spts", "scot", "sres", "sgrad", "rpts", "rcot", "rres", "rgrad"):
        names[name] = pltpu.VMEM(room, BF)
    for name in ("place", "pts", "cot", "res", "grad"):
        names["send" + name] = sent((PEERS,))
        names["recv" + name] = sent((PEERS,))
    for name, wide, piece in (
        ("a", 2 * FF, (rows, HALF)),
        ("b", 2 * C, (rows // 4, HALF)),
        ("c", 2 * C, (rows // 4, HALF)),
    ):
        for part in ("own", "got", "all"):
            names[name + part] = pltpu.VMEM((n_dp, rows, wide), BF)
        for part in ("cut", "cutgot", "fin"):
            names[name + part] = pltpu.VMEM((PEERS, *piece), F32)
        for step in range(4):
            names[f"{name}send{step}"] = sent((PEERS,))
            names[f"{name}recv{step}"] = sent((PEERS,))
    return names


class Scratch:
    def __init__(self, names, refs):
        for name, ref in zip(names, refs):
            setattr(self, name, ref)


def kernel(
    n_dp, names, tgt, pts, cot, w_qkv, w_out, w_up, w_down,
    res_out, grad_out, a_out, b_out, c_out, *refs,
):
    s = Scratch(names, refs)
    seq, zed = lax.axis_index("seq"), lax.axis_index("dp")
    barrier = pltpu.get_barrier_semaphore()
    for axis, size, me in (("seq", PEERS, seq), ("dp", n_dp, zed)):
        for d in range(1, size):
            pl.semaphore_signal(
                barrier,
                inc=1,
                device_id={axis: lax.rem(me + d, size)},
                device_id_type=pl.DeviceIdType.MESH,
            )

    def exchange(name, sign, source, target):
        return Copies(
            "seq", PEERS, seq, sign, lambda d, p: source.at[d], lambda d: target.at[d],
            getattr(s, "send" + name), getattr(s, "recv" + name),
        )

    go_place = exchange("place", 1, s.splace, s.place)
    go_pts = exchange("pts", 1, s.spts, s.rpts)
    go_cot = exchange("cot", 1, s.scot, s.rcot)
    go_res = exchange("res", -1, s.sres, s.rres)
    go_grad = exchange("grad", -1, s.sgrad, s.rgrad)

    slot, aux = slot_rows(tgt[...], seq)
    s.slot[...] = slot
    pl.semaphore_wait(barrier, PEERS - 1 + n_dp - 1)
    def pack(rows_ref, own_ref, sent_ref, go):
        for d in (4, 8, 12, 0):
            mine = one_hot(iota((4 * ROOM, ROWS), 0) + d * ROOM == slot)
            block = dot(mine, rows_ref[...]).astype(BF)
            for at in range(4):
                piece = block[at * ROOM : (at + 1) * ROOM]
                if d + at:
                    sent_ref[d + at] = piece
                    go.start(d + at)
                else:
                    own_ref[0] = piece

    pack(pts, s.rpts, s.spts, go_pts)
    for d in (4, 8, 12, 0):
        found = dot_nt(aux, one_hot(iota((4 * ROOM, ROWS), 0) + d * ROOM == slot))
        places = jnp.where(
            found[2:3] > 0.5, found[0:1] * 32.0 + found[1:2], float(ROWS)
        ).astype(jnp.int32)
        for at in range(4):
            place = jnp.broadcast_to(places[:, at * ROOM : (at + 1) * ROOM], (8, ROOM))
            if d + at:
                s.splace[d + at] = place
                go_place.start(d + at)
            else:
                s.place[0] = place
    pack(cot, s.rcot, s.scot, go_cot)

    def send_back(go, rows_ref, mine_ref, theirs_ref):
        rows = rows_ref[...]
        for d in (4, 8, 12, 0):
            cols = [
                column_of(s.place[d + at, 0:1, :].astype(F32)).astype(jnp.int32) for at in range(4)
            ]
            mine = one_hot(iota((4 * ROOM, ROWS), 1) == jnp.concatenate(cols, axis=0))
            block = dot(mine, rows).astype(BF)
            for at in range(4):
                piece = block[at * ROOM : (at + 1) * ROOM]
                if d + at:
                    theirs_ref[d + at] = piece
                    go.start(d + at)
                else:
                    mine_ref[0] = piece

    go_place.arrived()
    go_pts.arrived()
    place_rows(s, s.rpts, s.x)
    first_part(s, w_qkv)
    attend(s)
    for half in range(2):
        s.att[:, half * HALF : (half + 1) * HALF] = s.heads[half].astype(BF)
    s.ot[...] = transpose_bf(s.att[...])
    go_cot.arrived()
    place_rows(s, s.rcot, s.cot)
    feed_forward(s, w_out, w_up, w_down)
    send_back(go_res, s.out, s.rres, s.sres)

    wide, early, late = (Reduction(s, name, seq, zed, n_dp) for name in "abc")

    def put(ref, values, at):
        ref[:, :, at : at + values.shape[1]] = values.astype(BF).reshape(
            n_dp, C // n_dp, values.shape[1]
        )

    put(s.aown, dot(transpose_bf(s.second[...]), s.gexp[...]), 0)
    put(s.aown, dot(transpose_bf(s.cot[...]), s.act[...]), FF)
    wide.step0()
    out_grad = dot(s.ot[...], s.hrows[...])
    put(s.bown, out_grad[:, 0:HALF], 3 * HALF)
    put(s.cown, out_grad[:, HALF:C], 3 * HALF)

    def put_heads(ref, half):
        at = slice(half * HALF, (half + 1) * HALF)
        s.dq[:, at] = transpose_bf(s.dqt[at, :])
        for part, rows in enumerate((s.dq[:, at], s.dk[:, at].astype(BF), s.dv[:, at].astype(BF))):
            put(ref, dot(s.first_t[...], rows), part * HALF)

    prepare_back(s)

    def half_way():
        put_heads(s.bown, 0)
        early.step0()
        wide.step3()

    attend_back(
        s,
        {
            2: wide.step1,
            3: wide.step2,
            4: half_way,
            5: early.step1,
            6: early.step2,
            7: early.step3,
        },
    )
    put_heads(s.cown, 1)
    late.step0()
    g_first = dot_nt(s.dq[...], w_qkv[:, 0:C]) + dot_nt(s.dk[...].astype(BF), w_qkv[:, C : 2 * C])
    g_first = g_first + dot_nt(s.dv[...].astype(BF), w_qkv[:, 2 * C : 3 * C])
    normed, inverse = normalize(s.x[...].astype(F32))
    g_first = g_first.astype(BF).astype(F32)
    s.out[...] = (s.gh[...] + norm_back(normed, inverse, g_first)).astype(BF)
    go_res.sent()
    send_back(go_grad, s.out, s.rgrad, s.sgrad)
    late.step1()
    go_res.arrived()
    home_rows(s, s.rres, res_out)
    late.step2()
    wide.step4(a_out)
    late.step3()
    early.step4(b_out)
    go_grad.arrived()
    home_rows(s, s.rgrad, grad_out)
    late.step4(c_out)
    for go in (go_place, go_pts, go_cot, go_grad):
        go.sent()


def finish_kernel(factor, res, grad, a, b, c, res_out, grad_out, g_qkv, g_out, g_up, g_down, sems):
    first = pltpu.make_async_copy(res, res_out, sems.at[0])
    second = pltpu.make_async_copy(grad, grad_out, sems.at[1])
    first.start()
    second.start()
    g_up[...] = a[:, 0:FF].astype(F32) * factor
    for at in range(0, FF, C):
        g_down[at : at + C, :] = a[:, FF + at : FF + at + C].astype(F32).T * factor
    for half, ref in enumerate((b, c)):
        for part in range(3):
            at = part * C + half * HALF
            g_qkv[:, at : at + HALF] = ref[:, part * HALF : (part + 1) * HALF].astype(F32) * factor
        g_out[:, half * HALF : (half + 1) * HALF] = ref[:, 3 * HALF :].astype(F32) * factor
    first.wait()
    second.wait()


def body(points, targets, cotangent, w_qkv, w_out, w_up, w_down):
    n_dp = lax.axis_size("dp")
    factor = 1.0 / math.sqrt(points.shape[0] * n_dp * lax.axis_size("seq") * points.shape[1])
    names = scratch_of(n_dp)
    vmem = pl.BlockSpec(memory_space=pltpu.VMEM)
    rows_type = jax.ShapeDtypeStruct((ROWS, C), BF)
    gathered = pl.pallas_call(
        lambda *refs: kernel(n_dp, list(names), *refs),
        out_shape=[
            rows_type,
            rows_type,
            jax.ShapeDtypeStruct((C, 2 * FF), BF),
            jax.ShapeDtypeStruct((C, 2 * C), BF),
            jax.ShapeDtypeStruct((C, 2 * C), BF),
        ],
        in_specs=[vmem] * 7,
        out_specs=[vmem] * 5,
        scratch_shapes=list(names.values()),
        compiler_params=pltpu.CompilerParams(
            vmem_limit_bytes=60 * 1024 * 1024, collective_id=0, has_side_effects=True
        ),
    )(targets, points[0], cotangent[0], w_qkv, w_out, w_up, w_down)
    anywhere = pl.BlockSpec(memory_space=pl.ANY)
    result, grad_points, *grads = pl.pallas_call(
        lambda *refs: finish_kernel(factor, *refs),
        out_shape=[
            rows_type,
            rows_type,
            jax.ShapeDtypeStruct((C, 3 * C), F32),
            jax.ShapeDtypeStruct((C, C), F32),
            jax.ShapeDtypeStruct((C, FF), F32),
            jax.ShapeDtypeStruct((FF, C), F32),
        ],
        in_specs=[anywhere] * 2 + [vmem] * 3,
        out_specs=[anywhere] * 2 + [vmem] * 4,
        scratch_shapes=[pltpu.SemaphoreType.DMA((2,))],
    )(*gathered)
    return (result[None], grad_points[None], *grads)


def solution(mesh):
    return jax.shard_map(
        body,
        mesh=mesh,
        in_specs=(P("dp", "seq", None), P("dp", "seq"), P("dp", "seq", None), P(), P(), P(), P()),
        out_specs=(P("dp", "seq", None), P("dp", "seq", None), P(), P(), P(), P()),
        check_vma=False,
    )
```

```python
import math

import jax
import jax.numpy as jnp
from jax import lax
from jax.experimental import pallas as pl
from jax.experimental.pallas import tpu as pltpu
from jax.sharding import PartitionSpec as P

BF = jnp.bfloat16
F32 = jnp.float32
C = 256
HEADS = 16
DH = 16
FF = 1024
ROWS = 1024
PEERS = 16
ROOM = 128
SLOTS = PEERS * ROOM
BLK = 256
NB = ROWS // BLK
HALF = 128
EPS = 1e-05
GELU_A = 0.7978845608028654
GELU_B = 0.044715


def dot(left, right):
    return lax.dot_general(left, right, (((1,), (0,)), ((), ())), preferred_element_type=F32)


def dot_nt(left, right):
    return lax.dot_general(left, right, (((1,), (1,)), ((), ())), preferred_element_type=F32)


def iota(shape, axis):
    return lax.broadcasted_iota(jnp.int32, shape, axis)


def one_hot(cond):
    return jnp.where(cond, 1.0, 0.0).astype(BF)


def transpose_bf(values):
    return values.astype(F32).T.astype(BF)


def normalize(values):
    center = jnp.mean(values, axis=-1, keepdims=True)
    shifted = values - center
    inverse_std = lax.rsqrt(jnp.mean(shifted * shifted, axis=-1, keepdims=True) + EPS)
    return shifted * inverse_std, inverse_std


def norm_back(normed, inverse_std, upstream):
    return inverse_std * (
        upstream
        - jnp.mean(upstream, axis=-1, keepdims=True)
        - normed * jnp.mean(upstream * normed, axis=-1, keepdims=True)
    )


def gelu_pair(inputs):
    square = inputs * inputs
    tangent = jnp.tanh(GELU_A * (inputs + GELU_B * square * inputs))
    half = 0.5 * (1.0 + tangent)
    slopes = half + 0.5 * inputs * (1.0 - tangent * tangent) * GELU_A * (
        1.0 + 3.0 * GELU_B * square
    )
    return inputs * half, slopes


def column_of(row):
    return jnp.broadcast_to(row, (128, 128)).T[:, 0:1]


def slot_rows(targets, me):
    owner = lax.shift_right_logical(targets, 10)
    local = jnp.bitwise_and(targets, ROWS - 1)
    marks = iota((PEERS, ROWS), 0) == owner
    before = one_hot(iota((ROWS, ROWS), 0) < iota((ROWS, ROWS), 1))
    counts = dot(one_hot(marks), before)
    rank = jnp.sum(jnp.where(marks, counts, 0.0), axis=0, keepdims=True)
    slot = jnp.bitwise_and(owner - me, PEERS - 1) * ROOM + rank.astype(jnp.int32)
    part = iota((PEERS, ROWS), 0)
    aux = jnp.where(
        part == 0,
        lax.shift_right_logical(local, 5),
        jnp.where(part == 1, jnp.bitwise_and(local, 31), 1),
    )
    return slot, aux.astype(F32).astype(BF)


def home_rows(s, back, out_ref):
    rows = back[...].reshape(SLOTS, C)
    for block in range(ROWS // 128):
        at = slice(block * 128, (block + 1) * 128)
        col = column_of(s.slot[:, at].astype(F32)).astype(jnp.int32)
        out_ref[at, :] = dot(one_hot(iota((128, SLOTS), 1) == col), rows).astype(BF)


def place_rows(s, recv_ref, out_ref):
    recv = recv_ref[...].reshape(SLOTS, C)
    for block in range(NB):
        pieces = [
            one_hot(iota((BLK, ROOM), 0) + block * BLK == s.place[peer, 0:1, :])
            for peer in range(PEERS)
        ]
        out_ref[block * BLK : (block + 1) * BLK, :] = dot(
            jnp.concatenate(pieces, axis=1), recv
        ).astype(BF)


def first_part(s, w_ref):
    normed, _ = normalize(s.x[...].astype(F32))
    first = normed.astype(BF)
    s.first_t[...] = transpose_bf(first)
    qs = (dot(first, w_ref[:, 0:C]).astype(BF).astype(F32) * 0.25).astype(BF)
    k = dot(first, w_ref[:, C : 2 * C]).astype(BF)
    v = dot(first, w_ref[:, 2 * C : 3 * C]).astype(BF)
    s.q[...] = qs
    s.k[...] = k
    s.v[...] = v
    s.qt[...] = transpose_bf(qs)
    s.kt[...] = transpose_bf(k)
    for half in range(2):
        s.va[half, :, 0:HALF] = v[:, half * HALF : (half + 1) * HALF]
        s.va[half, :, HALF:C] = jnp.ones((ROWS, HALF), BF)
    s.za[...] = jnp.zeros((C, ROWS), BF)


def head_rows(h):
    return pl.ds(pl.multiple_of(h * DH, DH), DH)


def only_head(h, zeroed_ref, rows):
    zeroed_ref[head_rows(jnp.maximum(h - 1, 0)), :] = jnp.zeros((DH, ROWS), BF)
    zeroed_ref[head_rows(h), :] = rows


def attend(s):
    @pl.loop(0, HEADS, unroll=2)
    def _(h):
        half = h // 8
        only_head(h, s.za, s.kt[head_rows(h), :])
        lane = iota((HALF, HALF), 1)
        for block in range(ROWS // HALF):
            rows = slice(block * HALF, (block + 1) * HALF)
            scores = dot(s.q[rows, :], s.za[...])
            top = jnp.max(scores, axis=1, keepdims=True)
            out = dot(jnp.exp(scores - top).astype(BF), s.va[half])
            total = out[:, HALF : HALF + 1]
            s.heads[half, rows, :] = jnp.where(
                lax.shift_right_logical(lane, 4) == h - 8 * half,
                out[:, 0:HALF] * (1.0 / total),
                s.heads[half, rows, :],
            )
            s.lse[rows, :] = jnp.where(lane == h, top + jnp.log(total), s.lse[rows, :])


def feed_forward(s, w_out, w_up, w_down):
    @pl.loop(0, NB)
    def _(block):
        rows = pl.ds(pl.multiple_of(block * BLK, BLK), BLK)
        features = s.x[rows, :].astype(F32)
        tile_grad = s.cot[rows, :]
        hidden = features + dot(s.att[rows, :], w_out[...])
        normed, inverse = normalize(hidden)
        second = normed.astype(BF)
        s.second[rows, :] = second
        expanded = dot(second, w_up[...])
        activated, slopes = gelu_pair(expanded)
        activated = activated.astype(BF)
        s.act[rows, :] = activated
        s.out[rows, :] = (hidden + dot(activated, w_down[...])).astype(BF)
        gexp = (dot_nt(tile_grad, w_down[...]) * slopes).astype(BF)
        s.gexp[rows, :] = gexp
        grad_hidden = tile_grad.astype(F32) + norm_back(normed, inverse, dot_nt(gexp, w_up[...]))
        s.gh[rows, :] = grad_hidden
        hrows = grad_hidden.astype(BF)
        s.hrows[rows, :] = hrows
        s.datt[rows, :] = dot_nt(hrows, w_out[...]).astype(BF)


def prepare_back(s):
    dot_t = s.datt[...].astype(F32).T
    s.dot_t[...] = dot_t.astype(BF)
    inner = (dot_t * s.ot[...].astype(F32)).reshape(HEADS, DH, ROWS)
    s.inner[...] = jnp.sum(inner, axis=1, keepdims=True).reshape(HEADS, ROWS)
    s.lse_t[...] = s.lse[...].T[0:HEADS]
    s.za[...] = jnp.zeros((C, ROWS), BF)
    s.zb[...] = jnp.zeros((C, ROWS), BF)


def attend_back(s, steps):
    @pl.loop(0, HEADS // 2)
    def _(pair):
        for when, step in steps.items():
            pl.when(pair == when)(step)
        for odd in range(2):
            head_back(s, pair * 2 + odd)


def head_back(s, h):
    only_head(h, s.za, s.qt[head_rows(h), :])
    only_head(h, s.zb, s.dot_t[head_rows(h), :])
    keys = s.kt[head_rows(h), :]
    for block in range(NB):
        cols = slice(block * BLK, (block + 1) * BLK)
        probs = jnp.exp(dot(s.k[...], s.za[:, cols]) - s.lse_t[pl.ds(h, 1), cols])
        dp = dot(s.v[...], s.zb[:, cols])
        ds = (probs * (dp - s.inner[pl.ds(h, 1), cols])).astype(BF)
        s.p[:, cols] = probs.astype(BF)
        s.ds[:, cols] = ds
        s.dqt[head_rows(h), cols] = (dot(keys, ds) * 0.25).astype(BF)
    mine = lax.shift_right_logical(iota((ROWS, C), 1), 4) == h
    s.dv[...] = jnp.where(mine, dot(s.p[...], s.datt[...]), s.dv[...])
    s.dk[...] = jnp.where(mine, dot(s.ds[...], s.q[...]), s.dk[...])


class Copies:
    def __init__(self, axis, size, me, sign, source, target, send, recv):
        self.parts = {}
        for d in range(1, size):
            peer = lax.rem(me + (d if sign > 0 else size - d), size)
            self.parts[d] = pltpu.make_async_remote_copy(
                src_ref=source(d, peer),
                dst_ref=target(d),
                send_sem=send.at[d],
                recv_sem=recv.at[d],
                device_id={axis: peer},
                device_id_type=pl.DeviceIdType.MESH,
            )

    def start(self, d=None):
        for key, part in self.parts.items():
            if d is None or key == d:
                part.start()

    def arrived(self):
        for part in self.parts.values():
            part.wait_recv()

    def sent(self):
        for part in self.parts.values():
            part.wait_send()


class Reduction:
    def __init__(self, s, name, outer, inner):
        self.outer, self.inner = outer, inner
        self.own, self.got, self.cut, self.cut_got, self.fin, self.all = (
            getattr(s, name + part) for part in ("own", "got", "cut", "cutgot", "fin", "all")
        )
        sems = [(getattr(s, f"{name}send{i}"), getattr(s, f"{name}recv{i}")) for i in range(4)]
        at, to = outer[2], inner[2]
        self.first = lambda: Copies(
            *outer, 1, lambda d, p: self.own.at[p], lambda d: self.got.at[d], *sems[0]
        )
        self.second = lambda: Copies(
            *inner, 1, lambda d, p: self.cut.at[p], lambda d: self.cut_got.at[d], *sems[1]
        )
        self.third = lambda: Copies(
            *inner, 1, lambda d, p: self.fin.at[to], lambda d: self.fin.at[to], *sems[2]
        )
        self.fourth = lambda: Copies(
            *outer, 1, lambda d, p: self.all.at[at], lambda d: self.all.at[at], *sems[3]
        )

    def spots(self):
        rows, cols = self.cut.shape[1:]
        across = self.own.shape[2] // cols
        for piece in range(self.inner[1]):
            up, along = piece // across, piece % across
            yield piece, slice(up * rows, (up + 1) * rows), slice(along * cols, (along + 1) * cols)

    def step0(self):
        self.first().start()

    def step1(self):
        self.first().arrived()
        for piece, rows, cols in self.spots():
            total = self.own[self.outer[2], rows, cols].astype(F32)
            for d in range(1, self.outer[1]):
                total = total + self.got[d, rows, cols].astype(F32)
            self.cut[piece] = total
        self.second().start()

    def step2(self):
        self.second().arrived()
        total = self.cut[self.inner[2]]
        for d in range(1, self.inner[1]):
            total = total + self.cut_got[d]
        self.fin[self.inner[2]] = total
        self.third().start()

    def step3(self):
        self.third().arrived()
        across = self.own.shape[2] // self.cut.shape[2]
        bands = [
            jnp.concatenate([self.fin[at + piece] for piece in range(across)], axis=1)
            for at in range(0, self.inner[1], across)
        ]
        self.all[self.outer[2]] = jnp.concatenate(bands, axis=0).astype(BF)
        self.fourth().start()

    def step4(self, out_ref):
        self.fourth().arrived()
        out_ref[...] = self.all[...].reshape(out_ref.shape)
        for copies in (self.first, self.second, self.third, self.fourth):
            copies().sent()


def scratch_of(n_dp):
    rows = C // n_dp
    room, tall, flat, sent = (PEERS, ROOM, C), (ROWS, C), (C, ROWS), pltpu.SemaphoreType.DMA
    names = {}
    for name in ("x", "cot", "dq", "q", "k", "v", "att", "second", "hrows", "datt", "out"):
        names[name] = pltpu.VMEM(tall, BF)
    for name in ("gh", "dv", "dk"):
        names[name] = pltpu.VMEM(tall, F32)
    for name in ("first_t", "qt", "kt", "za", "zb", "ot", "dot_t", "dqt"):
        names[name] = pltpu.VMEM(flat, BF)
    for name in ("act", "gexp", "p", "ds"):
        names[name] = pltpu.VMEM((ROWS, FF), BF)
    for name in ("inner", "lse_t"):
        names[name] = pltpu.VMEM((HEADS, ROWS), F32)
    names["lse"] = pltpu.VMEM((ROWS, HALF), F32)
    names["va"] = pltpu.VMEM((2, ROWS, C), BF)
    names["heads"] = pltpu.VMEM((2, ROWS, HALF), F32)
    names["slot"] = pltpu.VMEM((1, ROWS), jnp.int32)
    for name in ("place", "splace"):
        names[name] = pltpu.VMEM((PEERS, 8, ROOM), jnp.int32)
    for name in ("spts", "scot", "sres", "sgrad", "rpts", "rcot", "rres", "rgrad"):
        names[name] = pltpu.VMEM(room, BF)
    for name in ("place", "pts", "cot", "res", "grad"):
        names["send" + name] = sent((PEERS,))
        names["recv" + name] = sent((PEERS,))
    for name, outer, inner, wide, piece in (
        ("a", n_dp, PEERS, 2 * FF, (rows, HALF)),
        ("b", n_dp, PEERS, 2 * C, (rows // 4, HALF)),
        ("c", PEERS, n_dp, 2 * C, (C // PEERS // min(2, n_dp), 2 * C * min(2, n_dp) // n_dp)),
    ):
        for part in ("own", "got", "all"):
            names[name + part] = pltpu.VMEM((outer, C // outer, wide), BF)
        for part in ("cut", "cutgot", "fin"):
            names[name + part] = pltpu.VMEM((inner, *piece), F32)
        for step in range(4):
            names[f"{name}send{step}"] = sent((PEERS,))
            names[f"{name}recv{step}"] = sent((PEERS,))
    return names


class Scratch:
    def __init__(self, names, refs):
        for name, ref in zip(names, refs):
            setattr(self, name, ref)


def kernel(
    n_dp, names, tgt, pts, cot, w_qkv, w_out, w_up, w_down,
    res_out, grad_out, a_out, b_out, c_out, *refs,
):
    s = Scratch(names, refs)
    seq, zed = lax.axis_index("seq"), lax.axis_index("dp")
    barrier = pltpu.get_barrier_semaphore()
    for axis, size, me in (("seq", PEERS, seq), ("dp", n_dp, zed)):
        for d in range(1, size):
            pl.semaphore_signal(
                barrier,
                inc=1,
                device_id={axis: lax.rem(me + d, size)},
                device_id_type=pl.DeviceIdType.MESH,
            )

    def exchange(name, sign, source, target):
        return Copies(
            "seq", PEERS, seq, sign, lambda d, p: source.at[d], lambda d: target.at[d],
            getattr(s, "send" + name), getattr(s, "recv" + name),
        )

    go_place = exchange("place", 1, s.splace, s.place)
    go_pts = exchange("pts", 1, s.spts, s.rpts)
    go_cot = exchange("cot", 1, s.scot, s.rcot)
    go_res = exchange("res", -1, s.sres, s.rres)
    go_grad = exchange("grad", -1, s.sgrad, s.rgrad)

    slot, aux = slot_rows(tgt[...], seq)
    s.slot[...] = slot
    pl.semaphore_wait(barrier, PEERS - 1 + n_dp - 1)
    def pack(rows_ref, own_ref, sent_ref, go):
        for d in (4, 8, 12, 0):
            mine = one_hot(iota((4 * ROOM, ROWS), 0) + d * ROOM == slot)
            block = dot(mine, rows_ref[...]).astype(BF)
            for at in range(4):
                piece = block[at * ROOM : (at + 1) * ROOM]
                if d + at:
                    sent_ref[d + at] = piece
                    if go is not None:
                        go.start(d + at)
                else:
                    own_ref[0] = piece

    pack(pts, s.rpts, s.spts, go_pts)
    for d in (4, 8, 12, 0):
        found = dot_nt(aux, one_hot(iota((4 * ROOM, ROWS), 0) + d * ROOM == slot))
        places = jnp.where(
            found[2:3] > 0.5, found[0:1] * 32.0 + found[1:2], float(ROWS)
        ).astype(jnp.int32)
        for at in range(4):
            place = jnp.broadcast_to(places[:, at * ROOM : (at + 1) * ROOM], (8, ROOM))
            if d + at:
                s.splace[d + at] = place
                go_place.start(d + at)
            else:
                s.place[0] = place
    pack(cot, s.rcot, s.scot, None)

    def send_back(go, rows_ref, mine_ref, theirs_ref):
        rows = rows_ref[...]
        for d in (4, 8, 12, 0):
            cols = [
                column_of(s.place[d + at, 0:1, :].astype(F32)).astype(jnp.int32) for at in range(4)
            ]
            mine = one_hot(iota((4 * ROOM, ROWS), 1) == jnp.concatenate(cols, axis=0))
            block = dot(mine, rows).astype(BF)
            for at in range(4):
                piece = block[at * ROOM : (at + 1) * ROOM]
                if d + at:
                    theirs_ref[d + at] = piece
                    go.start(d + at)
                else:
                    mine_ref[0] = piece

    go_place.arrived()
    go_pts.arrived()
    go_cot.start()
    place_rows(s, s.rpts, s.x)
    first_part(s, w_qkv)
    attend(s)
    for half in range(2):
        s.att[:, half * HALF : (half + 1) * HALF] = s.heads[half].astype(BF)
    s.ot[...] = transpose_bf(s.att[...])
    go_cot.arrived()
    place_rows(s, s.rcot, s.cot)
    feed_forward(s, w_out, w_up, w_down)
    send_back(go_res, s.out, s.rres, s.sres)

    along_seq, along_dp = ("seq", PEERS, seq), ("dp", n_dp, zed)
    wide = Reduction(s, "a", along_dp, along_seq)
    early = Reduction(s, "b", along_dp, along_seq)
    late = Reduction(s, "c", along_seq, along_dp)

    def put(ref, values, at):
        ref[:, :, at : at + values.shape[1]] = values.astype(BF).reshape(
            *ref.shape[0:2], values.shape[1]
        )

    put(s.aown, dot(transpose_bf(s.second[...]), s.gexp[...]), 0)
    put(s.aown, dot(transpose_bf(s.cot[...]), s.act[...]), FF)
    wide.step0()
    out_grad = dot(s.ot[...], s.hrows[...])
    put(s.bown, out_grad[:, 0:HALF], 3 * HALF)
    put(s.cown, out_grad[:, HALF:C], 3 * HALF)

    def put_heads(ref, half):
        at = slice(half * HALF, (half + 1) * HALF)
        s.dq[:, at] = transpose_bf(s.dqt[at, :])
        for part, rows in enumerate((s.dq[:, at], s.dk[:, at].astype(BF), s.dv[:, at].astype(BF))):
            put(ref, dot(s.first_t[...], rows), part * HALF)

    prepare_back(s)

    def half_way():
        put_heads(s.bown, 0)
        early.step0()
        wide.step3()

    attend_back(
        s,
        {
            2: wide.step1,
            3: wide.step2,
            4: half_way,
            5: early.step1,
            6: early.step2,
            7: early.step3,
        },
    )
    put_heads(s.cown, 1)
    late.step0()
    g_first = dot_nt(s.dq[...], w_qkv[:, 0:C]) + dot_nt(s.dk[...].astype(BF), w_qkv[:, C : 2 * C])
    g_first = g_first + dot_nt(s.dv[...].astype(BF), w_qkv[:, 2 * C : 3 * C])
    normed, inverse = normalize(s.x[...].astype(F32))
    g_first = g_first.astype(BF).astype(F32)
    s.out[...] = (s.gh[...] + norm_back(normed, inverse, g_first)).astype(BF)
    late.step1()
    send_back(go_grad, s.out, s.rgrad, s.sgrad)
    late.step2()
    go_res.arrived()
    home_rows(s, s.rres, res_out)
    late.step3()
    wide.step4(a_out)
    early.step4(b_out)
    go_grad.arrived()
    home_rows(s, s.rgrad, grad_out)
    late.step4(c_out)
    for go in (go_place, go_pts, go_cot, go_res, go_grad):
        go.sent()


def finish_kernel(factor, res, grad, a, b, c, res_out, grad_out, g_qkv, g_out, g_up, g_down):
    res_out[...] = res[...]
    grad_out[...] = grad[...]
    g_up[...] = a[:, 0:FF].astype(F32) * factor
    for at in range(0, FF, C):
        g_down[at : at + C, :] = a[:, FF + at : FF + at + C].astype(F32).T * factor
    for half, ref in enumerate((b, c)):
        for part in range(3):
            at = part * C + half * HALF
            g_qkv[:, at : at + HALF] = ref[:, part * HALF : (part + 1) * HALF].astype(F32) * factor
        g_out[:, half * HALF : (half + 1) * HALF] = ref[:, 3 * HALF :].astype(F32) * factor


def body(points, targets, cotangent, w_qkv, w_out, w_up, w_down):
    n_dp = lax.axis_size("dp")
    factor = 1.0 / math.sqrt(points.shape[0] * n_dp * lax.axis_size("seq") * points.shape[1])
    names = scratch_of(n_dp)
    vmem = pl.BlockSpec(memory_space=pltpu.VMEM)
    rows_type = jax.ShapeDtypeStruct((ROWS, C), BF)
    gathered = pl.pallas_call(
        lambda *refs: kernel(n_dp, list(names), *refs),
        out_shape=[
            rows_type,
            rows_type,
            jax.ShapeDtypeStruct((C, 2 * FF), BF),
            jax.ShapeDtypeStruct((C, 2 * C), BF),
            jax.ShapeDtypeStruct((C, 2 * C), BF),
        ],
        in_specs=[vmem] * 7,
        out_specs=[vmem] * 5,
        scratch_shapes=list(names.values()),
        compiler_params=pltpu.CompilerParams(
            vmem_limit_bytes=60 * 1024 * 1024, collective_id=0, has_side_effects=True
        ),
    )(targets, points[0], cotangent[0], w_qkv, w_out, w_up, w_down)
    result, grad_points, *grads = pl.pallas_call(
        lambda *refs: finish_kernel(factor, *refs),
        out_shape=[
            rows_type,
            rows_type,
            jax.ShapeDtypeStruct((C, 3 * C), F32),
            jax.ShapeDtypeStruct((C, C), F32),
            jax.ShapeDtypeStruct((C, FF), F32),
            jax.ShapeDtypeStruct((FF, C), F32),
        ],
        in_specs=[vmem] * 5,
        out_specs=[vmem] * 6,
    )(*gathered)
    return (result[None], grad_points[None], *grads)


def solution(mesh):
    return jax.shard_map(
        body,
        mesh=mesh,
        in_specs=(P("dp", "seq", None), P("dp", "seq"), P("dp", "seq", None), P(), P(), P(), P()),
        out_specs=(P("dp", "seq", None), P("dp", "seq", None), P(), P(), P(), P()),
        check_vma=False,
    )
```

```python
import math

import jax
import jax.numpy as jnp
from jax import lax
from jax.experimental import pallas as pl
from jax.experimental.pallas import tpu as pltpu
from jax.sharding import PartitionSpec as P

BF = jnp.bfloat16
F32 = jnp.float32
C = 256
HEADS = 16
DH = 16
FF = 1024
ROWS = 1024
PEERS = 16
ROOM = 128
SLOTS = PEERS * ROOM
BLK = 256
NB = ROWS // BLK
HALF = 128
EPS = 1e-05
GELU_A = 0.7978845608028654
GELU_B = 0.044715


def dot(left, right):
    return lax.dot_general(left, right, (((1,), (0,)), ((), ())), preferred_element_type=F32)


def dot_nt(left, right):
    return lax.dot_general(left, right, (((1,), (1,)), ((), ())), preferred_element_type=F32)


def iota(shape, axis):
    return lax.broadcasted_iota(jnp.int32, shape, axis)


def one_hot(cond):
    return jnp.where(cond, 1.0, 0.0).astype(BF)


def transpose_bf(values):
    return values.astype(F32).T.astype(BF)


def normalize(values):
    center = jnp.mean(values, axis=-1, keepdims=True)
    shifted = values - center
    inverse_std = lax.rsqrt(jnp.mean(shifted * shifted, axis=-1, keepdims=True) + EPS)
    return shifted * inverse_std, inverse_std


def norm_back(normed, inverse_std, upstream):
    return inverse_std * (
        upstream
        - jnp.mean(upstream, axis=-1, keepdims=True)
        - normed * jnp.mean(upstream * normed, axis=-1, keepdims=True)
    )


def gelu_pair(inputs):
    square = inputs * inputs
    tangent = jnp.tanh(GELU_A * (inputs + GELU_B * square * inputs))
    half = 0.5 * (1.0 + tangent)
    slopes = half + 0.5 * inputs * (1.0 - tangent * tangent) * GELU_A * (
        1.0 + 3.0 * GELU_B * square
    )
    return inputs * half, slopes


def column_of(row):
    return jnp.broadcast_to(row, (128, 128)).T[:, 0:1]


def slot_rows(targets, me):
    owner = lax.shift_right_logical(targets, 10)
    local = jnp.bitwise_and(targets, ROWS - 1)
    marks = iota((PEERS, ROWS), 0) == owner
    before = one_hot(iota((ROWS, ROWS), 0) < iota((ROWS, ROWS), 1))
    counts = dot(one_hot(marks), before)
    rank = jnp.sum(jnp.where(marks, counts, 0.0), axis=0, keepdims=True)
    slot = jnp.bitwise_and(owner - me, PEERS - 1) * ROOM + rank.astype(jnp.int32)
    part = iota((PEERS, ROWS), 0)
    aux = jnp.where(
        part == 0,
        lax.shift_right_logical(local, 5),
        jnp.where(part == 1, jnp.bitwise_and(local, 31), 1),
    )
    return slot, aux.astype(F32).astype(BF)


def home_rows(s, back, out_ref):
    rows = back[...].reshape(SLOTS, C)
    for block in range(ROWS // 128):
        at = slice(block * 128, (block + 1) * 128)
        col = column_of(s.slot[:, at].astype(F32)).astype(jnp.int32)
        out_ref[at, :] = dot(one_hot(iota((128, SLOTS), 1) == col), rows).astype(BF)


def place_rows(s, recv_ref, out_ref):
    recv = recv_ref[...].reshape(SLOTS, C)
    for block in range(NB):
        pieces = [
            one_hot(iota((BLK, ROOM), 0) + block * BLK == s.place[peer, 0:1, :])
            for peer in range(PEERS)
        ]
        out_ref[block * BLK : (block + 1) * BLK, :] = dot(
            jnp.concatenate(pieces, axis=1), recv
        ).astype(BF)


def first_part(s, w_ref):
    normed, _ = normalize(s.x[...].astype(F32))
    first = normed.astype(BF)
    s.first_t[...] = transpose_bf(first)
    qs = (dot(first, w_ref[:, 0:C]).astype(BF).astype(F32) * 0.25).astype(BF)
    k = dot(first, w_ref[:, C : 2 * C]).astype(BF)
    v = dot(first, w_ref[:, 2 * C : 3 * C]).astype(BF)
    s.q[...] = qs
    s.k[...] = k
    s.v[...] = v
    s.qt[...] = transpose_bf(qs)
    s.kt[...] = transpose_bf(k)
    for half in range(2):
        s.va[half, :, 0:HALF] = v[:, half * HALF : (half + 1) * HALF]
        s.va[half, :, HALF:C] = jnp.ones((ROWS, HALF), BF)
    s.za[...] = jnp.zeros((C, ROWS), BF)


def head_rows(h):
    return pl.ds(pl.multiple_of(h * DH, DH), DH)


def only_head(h, zeroed_ref, rows):
    zeroed_ref[head_rows(jnp.maximum(h - 1, 0)), :] = jnp.zeros((DH, ROWS), BF)
    zeroed_ref[head_rows(h), :] = rows


def attend(s):
    @pl.loop(0, HEADS, unroll=2)
    def _(h):
        half = h // 8
        only_head(h, s.za, s.kt[head_rows(h), :])
        lane = iota((HALF, HALF), 1)
        for block in range(ROWS // HALF):
            rows = slice(block * HALF, (block + 1) * HALF)
            scores = dot(s.q[rows, :], s.za[...])
            top = jnp.max(scores, axis=1, keepdims=True)
            out = dot(jnp.exp(scores - top).astype(BF), s.va[half])
            total = out[:, HALF : HALF + 1]
            s.heads[half, rows, :] = jnp.where(
                lax.shift_right_logical(lane, 4) == h - 8 * half,
                out[:, 0:HALF] * (1.0 / total),
                s.heads[half, rows, :],
            )
            s.lse[rows, :] = jnp.where(lane == h, top + jnp.log(total), s.lse[rows, :])


def feed_forward(s, w_out, w_up, w_down):
    @pl.loop(0, NB)
    def _(block):
        rows = pl.ds(pl.multiple_of(block * BLK, BLK), BLK)
        features = s.x[rows, :].astype(F32)
        tile_grad = s.cot[rows, :]
        hidden = features + dot(s.att[rows, :], w_out[...])
        normed, inverse = normalize(hidden)
        second = normed.astype(BF)
        s.second[rows, :] = second
        expanded = dot(second, w_up[...])
        activated, slopes = gelu_pair(expanded)
        activated = activated.astype(BF)
        s.act[rows, :] = activated
        s.out[rows, :] = (hidden + dot(activated, w_down[...])).astype(BF)
        gexp = (dot_nt(tile_grad, w_down[...]) * slopes).astype(BF)
        s.gexp[rows, :] = gexp
        grad_hidden = tile_grad.astype(F32) + norm_back(normed, inverse, dot_nt(gexp, w_up[...]))
        s.gh[rows, :] = grad_hidden
        hrows = grad_hidden.astype(BF)
        s.hrows[rows, :] = hrows
        s.datt[rows, :] = dot_nt(hrows, w_out[...]).astype(BF)


def prepare_back(s):
    dot_t = s.datt[...].astype(F32).T
    s.dot_t[...] = dot_t.astype(BF)
    inner = (dot_t * s.ot[...].astype(F32)).reshape(HEADS, DH, ROWS)
    s.inner[...] = jnp.sum(inner, axis=1, keepdims=True).reshape(HEADS, ROWS)
    s.lse_t[...] = s.lse[...].T[0:HEADS]
    s.za[...] = jnp.zeros((C, ROWS), BF)
    s.zb[...] = jnp.zeros((C, ROWS), BF)


def attend_back(s, steps):
    @pl.loop(0, HEADS // 2)
    def _(pair):
        for when, step in steps.items():
            pl.when(pair == when)(step)
        for odd in range(2):
            head_back(s, pair * 2 + odd)


def head_back(s, h):
    only_head(h, s.za, s.qt[head_rows(h), :])
    only_head(h, s.zb, s.dot_t[head_rows(h), :])
    keys = s.kt[head_rows(h), :]
    for block in range(NB):
        cols = slice(block * BLK, (block + 1) * BLK)
        probs = jnp.exp(dot(s.k[...], s.za[:, cols]) - s.lse_t[pl.ds(h, 1), cols])
        dp = dot(s.v[...], s.zb[:, cols])
        ds = (probs * (dp - s.inner[pl.ds(h, 1), cols])).astype(BF)
        s.p[:, cols] = probs.astype(BF)
        s.ds[:, cols] = ds
        s.dqt[head_rows(h), cols] = (dot(keys, ds) * 0.25).astype(BF)
    mine = lax.shift_right_logical(iota((ROWS, C), 1), 4) == h
    s.dv[...] = jnp.where(mine, dot(s.p[...], s.datt[...]), s.dv[...])
    s.dk[...] = jnp.where(mine, dot(s.ds[...], s.q[...]), s.dk[...])


class Copies:
    def __init__(self, axis, size, me, sign, source, target, send, recv):
        self.parts = {}
        for d in range(1, size):
            peer = lax.rem(me + (d if sign > 0 else size - d), size)
            self.parts[d] = pltpu.make_async_remote_copy(
                src_ref=source(d, peer),
                dst_ref=target(d),
                send_sem=send.at[d],
                recv_sem=recv.at[d],
                device_id={axis: peer},
                device_id_type=pl.DeviceIdType.MESH,
            )

    def start(self, d=None):
        for key, part in self.parts.items():
            if d is None or key == d:
                part.start()

    def arrived(self):
        for part in self.parts.values():
            part.wait_recv()

    def sent(self):
        for part in self.parts.values():
            part.wait_send()


class Reduction:
    def __init__(self, s, name, outer, inner):
        self.outer, self.inner = outer, inner
        self.own, self.got, self.cut, self.cut_got, self.fin, self.all = (
            getattr(s, name + part) for part in ("own", "got", "cut", "cutgot", "fin", "all")
        )
        sems = [(getattr(s, f"{name}send{i}"), getattr(s, f"{name}recv{i}")) for i in range(4)]
        at, to = outer[2], inner[2]
        self.first = lambda: Copies(
            *outer, 1, lambda d, p: self.own.at[p], lambda d: self.got.at[d], *sems[0]
        )
        self.second = lambda: Copies(
            *inner, 1, lambda d, p: self.cut.at[p], lambda d: self.cut_got.at[d], *sems[1]
        )
        self.third = lambda: Copies(
            *inner, 1, lambda d, p: self.fin.at[to], lambda d: self.fin.at[to], *sems[2]
        )
        self.fourth = lambda: Copies(
            *outer, 1, lambda d, p: self.all.at[at], lambda d: self.all.at[at], *sems[3]
        )

    def spots(self):
        rows, cols = self.cut.shape[1:]
        across = self.own.shape[2] // cols
        for piece in range(self.inner[1]):
            up, along = piece // across, piece % across
            yield piece, slice(up * rows, (up + 1) * rows), slice(along * cols, (along + 1) * cols)

    def step0(self):
        self.first().start()

    def step1(self):
        self.first().arrived()
        for piece, rows, cols in self.spots():
            total = self.own[self.outer[2], rows, cols].astype(F32)
            for d in range(1, self.outer[1]):
                total = total + self.got[d, rows, cols].astype(F32)
            self.cut[piece] = total
        self.second().start()

    def step2(self):
        self.second().arrived()
        total = self.cut[self.inner[2]]
        for d in range(1, self.inner[1]):
            total = total + self.cut_got[d]
        self.fin[self.inner[2]] = total
        self.third().start()

    def step3(self):
        self.third().arrived()
        across = self.own.shape[2] // self.cut.shape[2]
        bands = [
            jnp.concatenate([self.fin[at + piece] for piece in range(across)], axis=1)
            for at in range(0, self.inner[1], across)
        ]
        self.all[self.outer[2]] = jnp.concatenate(bands, axis=0).astype(BF)
        self.fourth().start()

    def step4(self, out_ref):
        self.fourth().arrived()
        out_ref[...] = self.all[...].reshape(out_ref.shape)
        for copies in (self.first, self.second, self.third, self.fourth):
            copies().sent()


class ShortReduction:
    def __init__(self, s, name, seq, zed, n_dp):
        self.seq, self.zed, self.n_dp = seq, zed, n_dp
        self.own, self.got, self.mid, self.all = (
            getattr(s, name + part) for part in ("own", "got", "mid", "all")
        )
        sems = [(getattr(s, f"{name}send{i}"), getattr(s, f"{name}recv{i}")) for i in range(3)]
        self.first = lambda: Copies(
            "seq", PEERS, seq, 1, lambda d, p: self.own.at[p], lambda d: self.got.at[d], *sems[0]
        )
        self.second = lambda: Copies(
            "dp", n_dp, zed, 1, lambda d, p: self.mid.at[zed], lambda d: self.mid.at[zed], *sems[1]
        )
        self.third = lambda: Copies(
            "seq", PEERS, seq, 1, lambda d, p: self.all.at[seq], lambda d: self.all.at[seq], *sems[2]
        )

    def step0(self):
        self.first().start()

    def step1(self):
        self.first().arrived()
        total = self.own[self.seq].astype(F32)
        for d in range(1, PEERS):
            total = total + self.got[d].astype(F32)
        self.mid[self.zed] = total.astype(BF)
        self.second().start()

    def step2(self):
        self.second().arrived()
        total = self.mid[0].astype(F32)
        for other in range(1, self.n_dp):
            total = total + self.mid[other].astype(F32)
        self.all[self.seq] = total.astype(BF)
        self.third().start()

    def step3(self, out_ref):
        self.third().arrived()
        out_ref[...] = self.all[...].reshape(out_ref.shape)
        for copies in (self.first, self.second, self.third):
            copies().sent()


def scratch_of(n_dp):
    rows = C // n_dp
    room, tall, flat, sent = (PEERS, ROOM, C), (ROWS, C), (C, ROWS), pltpu.SemaphoreType.DMA
    names = {}
    for name in ("x", "cot", "dq", "q", "k", "v", "att", "second", "hrows", "datt", "out"):
        names[name] = pltpu.VMEM(tall, BF)
    for name in ("gh", "dv", "dk"):
        names[name] = pltpu.VMEM(tall, F32)
    for name in ("first_t", "qt", "kt", "za", "zb", "ot", "dot_t", "dqt"):
        names[name] = pltpu.VMEM(flat, BF)
    for name in ("act", "gexp", "p", "ds"):
        names[name] = pltpu.VMEM((ROWS, FF), BF)
    for name in ("inner", "lse_t"):
        names[name] = pltpu.VMEM((HEADS, ROWS), F32)
    names["lse"] = pltpu.VMEM((ROWS, HALF), F32)
    names["va"] = pltpu.VMEM((2, ROWS, C), BF)
    names["heads"] = pltpu.VMEM((2, ROWS, HALF), F32)
    names["slot"] = pltpu.VMEM((1, ROWS), jnp.int32)
    for name in ("place", "splace"):
        names[name] = pltpu.VMEM((PEERS, 8, ROOM), jnp.int32)
    for name in ("spts", "scot", "sres", "sgrad", "rpts", "rcot", "rres", "rgrad"):
        names[name] = pltpu.VMEM(room, BF)
    for name in ("place", "pts", "cot", "res", "grad"):
        names["send" + name] = sent((PEERS,))
        names["recv" + name] = sent((PEERS,))
    for name, outer, inner, wide, piece in (
        ("a", n_dp, PEERS, 2 * FF, (rows, HALF)),
        ("b", n_dp, PEERS, 2 * C, (rows // 4, HALF)),
    ):
        for part in ("own", "got", "all"):
            names[name + part] = pltpu.VMEM((outer, C // outer, wide), BF)
        for part in ("cut", "cutgot", "fin"):
            names[name + part] = pltpu.VMEM((inner, *piece), F32)
        for step in range(4):
            names[f"{name}send{step}"] = sent((PEERS,))
            names[f"{name}recv{step}"] = sent((PEERS,))
    for part in ("own", "got", "all"):
        names["c" + part] = pltpu.VMEM((PEERS, C // PEERS, 2 * C), BF)
    names["cmid"] = pltpu.VMEM((n_dp, C // PEERS, 2 * C), BF)
    for step in range(3):
        names[f"csend{step}"] = sent((PEERS,))
        names[f"crecv{step}"] = sent((PEERS,))
    return names


class Scratch:
    def __init__(self, names, refs):
        for name, ref in zip(names, refs):
            setattr(self, name, ref)


def kernel(
    n_dp, names, tgt, pts, cot, w_qkv, w_out, w_up, w_down,
    res_out, grad_out, a_out, b_out, c_out, *refs,
):
    s = Scratch(names, refs)
    seq, zed = lax.axis_index("seq"), lax.axis_index("dp")
    barrier = pltpu.get_barrier_semaphore()
    for axis, size, me in (("seq", PEERS, seq), ("dp", n_dp, zed)):
        for d in range(1, size):
            pl.semaphore_signal(
                barrier,
                inc=1,
                device_id={axis: lax.rem(me + d, size)},
                device_id_type=pl.DeviceIdType.MESH,
            )

    def exchange(name, sign, source, target):
        return Copies(
            "seq", PEERS, seq, sign, lambda d, p: source.at[d], lambda d: target.at[d],
            getattr(s, "send" + name), getattr(s, "recv" + name),
        )

    go_place = exchange("place", 1, s.splace, s.place)
    go_pts = exchange("pts", 1, s.spts, s.rpts)
    go_cot = exchange("cot", 1, s.scot, s.rcot)
    go_res = exchange("res", -1, s.sres, s.rres)
    go_grad = exchange("grad", -1, s.sgrad, s.rgrad)

    slot, aux = slot_rows(tgt[...], seq)
    s.slot[...] = slot
    pl.semaphore_wait(barrier, PEERS - 1 + n_dp - 1)
    def pack(rows_ref, own_ref, sent_ref, go):
        for d in (4, 8, 12, 0):
            mine = one_hot(iota((4 * ROOM, ROWS), 0) + d * ROOM == slot)
            block = dot(mine, rows_ref[...]).astype(BF)
            for at in range(4):
                piece = block[at * ROOM : (at + 1) * ROOM]
                if d + at:
                    sent_ref[d + at] = piece
                    if go is not None:
                        go.start(d + at)
                else:
                    own_ref[0] = piece

    pack(pts, s.rpts, s.spts, go_pts)
    for d in (4, 8, 12, 0):
        found = dot_nt(aux, one_hot(iota((4 * ROOM, ROWS), 0) + d * ROOM == slot))
        places = jnp.where(
            found[2:3] > 0.5, found[0:1] * 32.0 + found[1:2], float(ROWS)
        ).astype(jnp.int32)
        for at in range(4):
            place = jnp.broadcast_to(places[:, at * ROOM : (at + 1) * ROOM], (8, ROOM))
            if d + at:
                s.splace[d + at] = place
                go_place.start(d + at)
            else:
                s.place[0] = place
    pack(cot, s.rcot, s.scot, None)

    def send_back(go, rows_ref, mine_ref, theirs_ref):
        rows = rows_ref[...]
        for d in (4, 8, 12, 0):
            cols = [
                column_of(s.place[d + at, 0:1, :].astype(F32)).astype(jnp.int32) for at in range(4)
            ]
            mine = one_hot(iota((4 * ROOM, ROWS), 1) == jnp.concatenate(cols, axis=0))
            block = dot(mine, rows).astype(BF)
            for at in range(4):
                piece = block[at * ROOM : (at + 1) * ROOM]
                if d + at:
                    theirs_ref[d + at] = piece
                    go.start(d + at)
                else:
                    mine_ref[0] = piece

    go_place.arrived()
    go_pts.arrived()
    go_cot.start()
    place_rows(s, s.rpts, s.x)
    first_part(s, w_qkv)
    attend(s)
    for half in range(2):
        s.att[:, half * HALF : (half + 1) * HALF] = s.heads[half].astype(BF)
    s.ot[...] = transpose_bf(s.att[...])
    go_cot.arrived()
    place_rows(s, s.rcot, s.cot)
    feed_forward(s, w_out, w_up, w_down)
    send_back(go_res, s.out, s.rres, s.sres)

    along_seq, along_dp = ("seq", PEERS, seq), ("dp", n_dp, zed)
    wide = Reduction(s, "a", along_dp, along_seq)
    early = Reduction(s, "b", along_dp, along_seq)
    late = ShortReduction(s, "c", seq, zed, n_dp)

    def put(ref, values, at):
        ref[:, :, at : at + values.shape[1]] = values.astype(BF).reshape(
            *ref.shape[0:2], values.shape[1]
        )

    put(s.aown, dot(transpose_bf(s.second[...]), s.gexp[...]), 0)
    put(s.aown, dot(transpose_bf(s.cot[...]), s.act[...]), FF)
    wide.step0()
    out_grad = dot(s.ot[...], s.hrows[...])
    put(s.bown, out_grad[:, 0:HALF], 3 * HALF)
    put(s.cown, out_grad[:, HALF:C], 3 * HALF)

    def put_heads(ref, half):
        at = slice(half * HALF, (half + 1) * HALF)
        s.dq[:, at] = transpose_bf(s.dqt[at, :])
        for part, rows in enumerate((s.dq[:, at], s.dk[:, at].astype(BF), s.dv[:, at].astype(BF))):
            put(ref, dot(s.first_t[...], rows), part * HALF)

    prepare_back(s)

    def half_way():
        put_heads(s.bown, 0)
        early.step0()
        wide.step3()

    attend_back(
        s,
        {
            2: wide.step1,
            3: wide.step2,
            4: half_way,
            5: early.step1,
            6: early.step2,
            7: early.step3,
        },
    )
    put_heads(s.cown, 1)
    late.step0()
    g_first = dot_nt(s.dq[...], w_qkv[:, 0:C]) + dot_nt(s.dk[...].astype(BF), w_qkv[:, C : 2 * C])
    g_first = g_first + dot_nt(s.dv[...].astype(BF), w_qkv[:, 2 * C : 3 * C])
    normed, inverse = normalize(s.x[...].astype(F32))
    g_first = g_first.astype(BF).astype(F32)
    s.out[...] = (s.gh[...] + norm_back(normed, inverse, g_first)).astype(BF)
    send_back(go_grad, s.out, s.rgrad, s.sgrad)
    late.step1()
    go_res.arrived()
    home_rows(s, s.rres, res_out)
    late.step2()
    wide.step4(a_out)
    early.step4(b_out)
    go_grad.arrived()
    home_rows(s, s.rgrad, grad_out)
    late.step3(c_out)
    for go in (go_place, go_pts, go_cot, go_res, go_grad):
        go.sent()


def finish_kernel(factor, res, grad, a, b, c, res_out, grad_out, g_qkv, g_out, g_up, g_down):
    res_out[...] = res[...]
    grad_out[...] = grad[...]
    g_up[...] = a[:, 0:FF].astype(F32) * factor
    for at in range(0, FF, C):
        g_down[at : at + C, :] = a[:, FF + at : FF + at + C].astype(F32).T * factor
    for half, ref in enumerate((b, c)):
        for part in range(3):
            at = part * C + half * HALF
            g_qkv[:, at : at + HALF] = ref[:, part * HALF : (part + 1) * HALF].astype(F32) * factor
        g_out[:, half * HALF : (half + 1) * HALF] = ref[:, 3 * HALF :].astype(F32) * factor


def body(points, targets, cotangent, w_qkv, w_out, w_up, w_down):
    n_dp = lax.axis_size("dp")
    factor = 1.0 / math.sqrt(points.shape[0] * n_dp * lax.axis_size("seq") * points.shape[1])
    names = scratch_of(n_dp)
    vmem = pl.BlockSpec(memory_space=pltpu.VMEM)
    rows_type = jax.ShapeDtypeStruct((ROWS, C), BF)
    gathered = pl.pallas_call(
        lambda *refs: kernel(n_dp, list(names), *refs),
        out_shape=[
            rows_type,
            rows_type,
            jax.ShapeDtypeStruct((C, 2 * FF), BF),
            jax.ShapeDtypeStruct((C, 2 * C), BF),
            jax.ShapeDtypeStruct((C, 2 * C), BF),
        ],
        in_specs=[vmem] * 7,
        out_specs=[vmem] * 5,
        scratch_shapes=list(names.values()),
        compiler_params=pltpu.CompilerParams(
            vmem_limit_bytes=60 * 1024 * 1024, collective_id=0, has_side_effects=True
        ),
    )(targets, points[0], cotangent[0], w_qkv, w_out, w_up, w_down)
    result, grad_points, *grads = pl.pallas_call(
        lambda *refs: finish_kernel(factor, *refs),
        out_shape=[
            rows_type,
            rows_type,
            jax.ShapeDtypeStruct((C, 3 * C), F32),
            jax.ShapeDtypeStruct((C, C), F32),
            jax.ShapeDtypeStruct((C, FF), F32),
            jax.ShapeDtypeStruct((FF, C), F32),
        ],
        in_specs=[vmem] * 5,
        out_specs=[vmem] * 6,
    )(*gathered)
    return (result[None], grad_points[None], *grads)


def solution(mesh):
    return jax.shard_map(
        body,
        mesh=mesh,
        in_specs=(P("dp", "seq", None), P("dp", "seq"), P("dp", "seq", None), P(), P(), P(), P()),
        out_specs=(P("dp", "seq", None), P("dp", "seq", None), P(), P(), P(), P()),
        check_vma=False,
    )
```

```python
import math

import jax
import jax.numpy as jnp
from jax import lax
from jax.experimental import pallas as pl
from jax.experimental.pallas import tpu as pltpu
from jax.sharding import PartitionSpec as P

BF = jnp.bfloat16
F32 = jnp.float32
C = 256
HEADS = 16
DH = 16
FF = 1024
ROWS = 1024
PEERS = 16
ROOM = 128
SLOTS = PEERS * ROOM
BLK = 256
NB = ROWS // BLK
HALF = 128
EPS = 1e-05
GELU_A = 0.7978845608028654
GELU_B = 0.044715


def dot(left, right):
    return lax.dot_general(left, right, (((1,), (0,)), ((), ())), preferred_element_type=F32)


def dot_nt(left, right):
    return lax.dot_general(left, right, (((1,), (1,)), ((), ())), preferred_element_type=F32)


def iota(shape, axis):
    return lax.broadcasted_iota(jnp.int32, shape, axis)


def one_hot(cond):
    return jnp.where(cond, 1.0, 0.0).astype(BF)


def transpose_bf(values):
    return values.astype(F32).T.astype(BF)


def normalize(values):
    center = jnp.mean(values, axis=-1, keepdims=True)
    shifted = values - center
    inverse_std = lax.rsqrt(jnp.mean(shifted * shifted, axis=-1, keepdims=True) + EPS)
    return shifted * inverse_std, inverse_std


def norm_back(normed, inverse_std, upstream):
    return inverse_std * (
        upstream
        - jnp.mean(upstream, axis=-1, keepdims=True)
        - normed * jnp.mean(upstream * normed, axis=-1, keepdims=True)
    )


def gelu_pair(inputs):
    square = inputs * inputs
    tangent = jnp.tanh(GELU_A * (inputs + GELU_B * square * inputs))
    half = 0.5 * (1.0 + tangent)
    slopes = half + 0.5 * inputs * (1.0 - tangent * tangent) * GELU_A * (
        1.0 + 3.0 * GELU_B * square
    )
    return inputs * half, slopes


def column_of(row):
    return jnp.broadcast_to(row, (128, 128)).T[:, 0:1]


def slot_rows(targets, me):
    owner = lax.shift_right_logical(targets, 10)
    local = jnp.bitwise_and(targets, ROWS - 1)
    marks = iota((PEERS, ROWS), 0) == owner
    before = one_hot(iota((ROWS, ROWS), 0) < iota((ROWS, ROWS), 1))
    counts = dot(one_hot(marks), before)
    rank = jnp.sum(jnp.where(marks, counts, 0.0), axis=0, keepdims=True)
    slot = jnp.bitwise_and(owner - me, PEERS - 1) * ROOM + rank.astype(jnp.int32)
    part = iota((PEERS, ROWS), 0)
    aux = jnp.where(
        part == 0,
        lax.shift_right_logical(local, 5),
        jnp.where(part == 1, jnp.bitwise_and(local, 31), 1),
    )
    return slot, aux.astype(F32).astype(BF)


def home_rows(s, back, out_ref):
    rows = back[...].reshape(SLOTS, C)
    for block in range(ROWS // 128):
        at = slice(block * 128, (block + 1) * 128)
        col = column_of(s.slot[:, at].astype(F32)).astype(jnp.int32)
        out_ref[at, :] = dot(one_hot(iota((128, SLOTS), 1) == col), rows).astype(BF)


def place_rows(s, recv_ref, out_ref):
    recv = recv_ref[...].reshape(SLOTS, C)
    for block in range(NB):
        pieces = [
            one_hot(iota((BLK, ROOM), 0) + block * BLK == s.place[peer, 0:1, :])
            for peer in range(PEERS)
        ]
        out_ref[block * BLK : (block + 1) * BLK, :] = dot(
            jnp.concatenate(pieces, axis=1), recv
        ).astype(BF)


def first_part(s, w_ref):
    normed, _ = normalize(s.x[...].astype(F32))
    first = normed.astype(BF)
    s.first_t[...] = transpose_bf(first)
    qs = (dot(first, w_ref[:, 0:C]).astype(BF).astype(F32) * 0.25).astype(BF)
    k = dot(first, w_ref[:, C : 2 * C]).astype(BF)
    v = dot(first, w_ref[:, 2 * C : 3 * C]).astype(BF)
    s.q[...] = qs
    s.k[...] = k
    s.v[...] = v
    s.qt[...] = transpose_bf(qs)
    s.kt[...] = transpose_bf(k)
    for half in range(2):
        s.va[half, :, 0:HALF] = v[:, half * HALF : (half + 1) * HALF]
        s.va[half, :, HALF:C] = jnp.ones((ROWS, HALF), BF)
    s.za[...] = jnp.zeros((C, ROWS), BF)


def head_rows(h):
    return pl.ds(pl.multiple_of(h * DH, DH), DH)


def only_head(h, zeroed_ref, rows):
    zeroed_ref[head_rows(jnp.maximum(h - 1, 0)), :] = jnp.zeros((DH, ROWS), BF)
    zeroed_ref[head_rows(h), :] = rows


def attend(s):
    @pl.loop(0, HEADS, unroll=2)
    def _(h):
        half = h // 8
        only_head(h, s.za, s.kt[head_rows(h), :])
        lane = iota((HALF, HALF), 1)
        for block in range(ROWS // HALF):
            rows = slice(block * HALF, (block + 1) * HALF)
            scores = dot(s.q[rows, :], s.za[...])
            top = jnp.max(scores, axis=1, keepdims=True)
            out = dot(jnp.exp(scores - top).astype(BF), s.va[half])
            total = out[:, HALF : HALF + 1]
            s.heads[half, rows, :] = jnp.where(
                lax.shift_right_logical(lane, 4) == h - 8 * half,
                out[:, 0:HALF] * (1.0 / total),
                s.heads[half, rows, :],
            )
            s.lse[rows, :] = jnp.where(lane == h, top + jnp.log(total), s.lse[rows, :])


def feed_forward(s, w_out, w_up, w_down):
    @pl.loop(0, NB)
    def _(block):
        rows = pl.ds(pl.multiple_of(block * BLK, BLK), BLK)
        features = s.x[rows, :].astype(F32)
        tile_grad = s.cot[rows, :]
        hidden = features + dot(s.att[rows, :], w_out[...])
        normed, inverse = normalize(hidden)
        second = normed.astype(BF)
        s.second[rows, :] = second
        expanded = dot(second, w_up[...])
        activated, slopes = gelu_pair(expanded)
        activated = activated.astype(BF)
        s.act[rows, :] = activated
        s.out[rows, :] = (hidden + dot(activated, w_down[...])).astype(BF)
        gexp = (dot_nt(tile_grad, w_down[...]) * slopes).astype(BF)
        s.gexp[rows, :] = gexp
        grad_hidden = tile_grad.astype(F32) + norm_back(normed, inverse, dot_nt(gexp, w_up[...]))
        s.gh[rows, :] = grad_hidden
        hrows = grad_hidden.astype(BF)
        s.hrows[rows, :] = hrows
        s.datt[rows, :] = dot_nt(hrows, w_out[...]).astype(BF)


def prepare_back(s):
    dot_t = s.datt[...].astype(F32).T
    s.dot_t[...] = dot_t.astype(BF)
    inner = (dot_t * s.ot[...].astype(F32)).reshape(HEADS, DH, ROWS)
    s.inner[...] = jnp.sum(inner, axis=1, keepdims=True).reshape(HEADS, ROWS)
    s.lse_t[...] = s.lse[...].T[0:HEADS]
    s.za[...] = jnp.zeros((C, ROWS), BF)
    s.zb[...] = jnp.zeros((C, ROWS), BF)


def attend_back(s, steps):
    @pl.loop(0, HEADS // 2)
    def _(pair):
        for when, step in steps.items():
            pl.when(pair == when)(step)
        for odd in range(2):
            head_back(s, pair * 2 + odd)


def head_back(s, h):
    only_head(h, s.za, s.qt[head_rows(h), :])
    only_head(h, s.zb, s.dot_t[head_rows(h), :])
    keys = s.kt[head_rows(h), :]
    for block in range(NB):
        cols = slice(block * BLK, (block + 1) * BLK)
        probs = jnp.exp(dot(s.k[...], s.za[:, cols]) - s.lse_t[pl.ds(h, 1), cols])
        dp = dot(s.v[...], s.zb[:, cols])
        ds = (probs * (dp - s.inner[pl.ds(h, 1), cols])).astype(BF)
        s.p[:, cols] = probs.astype(BF)
        s.ds[:, cols] = ds
        s.dqt[head_rows(h), cols] = (dot(keys, ds) * 0.25).astype(BF)
    mine = lax.shift_right_logical(iota((ROWS, C), 1), 4) == h
    s.dv[...] = jnp.where(mine, dot(s.p[...], s.datt[...]), s.dv[...])
    s.dk[...] = jnp.where(mine, dot(s.ds[...], s.q[...]), s.dk[...])


class Copies:
    def __init__(self, axis, size, me, sign, source, target, send, recv):
        self.parts = {}
        for d in range(1, size):
            peer = lax.rem(me + (d if sign > 0 else size - d), size)
            self.parts[d] = pltpu.make_async_remote_copy(
                src_ref=source(d, peer),
                dst_ref=target(d),
                send_sem=send.at[d],
                recv_sem=recv.at[d],
                device_id={axis: peer},
                device_id_type=pl.DeviceIdType.MESH,
            )

    def start(self, d=None):
        for key, part in self.parts.items():
            if d is None or key == d:
                part.start()

    def arrived(self):
        for part in self.parts.values():
            part.wait_recv()

    def sent(self):
        for part in self.parts.values():
            part.wait_send()


class Reduction:
    def __init__(self, s, name, outer, inner):
        self.outer, self.inner = outer, inner
        self.own, self.got, self.cut, self.cut_got, self.fin, self.all = (
            getattr(s, name + part) for part in ("own", "got", "cut", "cutgot", "fin", "all")
        )
        sems = [(getattr(s, f"{name}send{i}"), getattr(s, f"{name}recv{i}")) for i in range(4)]
        at, to = outer[2], inner[2]
        self.first = lambda: Copies(
            *outer, 1, lambda d, p: self.own.at[p], lambda d: self.got.at[d], *sems[0]
        )
        self.second = lambda: Copies(
            *inner, 1, lambda d, p: self.cut.at[p], lambda d: self.cut_got.at[d], *sems[1]
        )
        self.third = lambda: Copies(
            *inner, 1, lambda d, p: self.fin.at[to], lambda d: self.fin.at[to], *sems[2]
        )
        self.fourth = lambda: Copies(
            *outer, 1, lambda d, p: self.all.at[at], lambda d: self.all.at[at], *sems[3]
        )

    def spots(self):
        rows, cols = self.cut.shape[1:]
        across = self.own.shape[2] // cols
        for piece in range(self.inner[1]):
            up, along = piece // across, piece % across
            yield piece, slice(up * rows, (up + 1) * rows), slice(along * cols, (along + 1) * cols)

    def step0(self):
        self.first().start()

    def step1(self):
        self.first().arrived()
        for piece, rows, cols in self.spots():
            total = self.own[self.outer[2], rows, cols].astype(F32)
            for d in range(1, self.outer[1]):
                total = total + self.got[d, rows, cols].astype(F32)
            self.cut[piece] = total
        self.second().start()

    def step2(self):
        self.second().arrived()
        total = self.cut[self.inner[2]]
        for d in range(1, self.inner[1]):
            total = total + self.cut_got[d]
        self.fin[self.inner[2]] = total
        self.third().start()

    def step3(self):
        self.third().arrived()
        across = self.own.shape[2] // self.cut.shape[2]
        bands = [
            jnp.concatenate([self.fin[at + piece] for piece in range(across)], axis=1)
            for at in range(0, self.inner[1], across)
        ]
        self.all[self.outer[2]] = jnp.concatenate(bands, axis=0).astype(BF)
        self.fourth().start()

    def step4(self, out_ref):
        self.fourth().arrived()
        out_ref[...] = self.all[...].reshape(out_ref.shape)
        for copies in (self.first, self.second, self.third, self.fourth):
            copies().sent()


def scratch_of(n_dp):
    rows = C // n_dp
    room, tall, flat, sent = (PEERS, ROOM, C), (ROWS, C), (C, ROWS), pltpu.SemaphoreType.DMA
    names = {}
    for name in ("x", "cot", "dq", "q", "k", "v", "att", "second", "hrows", "datt", "out"):
        names[name] = pltpu.VMEM(tall, BF)
    for name in ("gh", "dv", "dk"):
        names[name] = pltpu.VMEM(tall, F32)
    for name in ("first_t", "qt", "kt", "za", "zb", "ot", "dot_t", "dqt"):
        names[name] = pltpu.VMEM(flat, BF)
    for name in ("act", "gexp", "p", "ds"):
        names[name] = pltpu.VMEM((ROWS, FF), BF)
    for name in ("inner", "lse_t"):
        names[name] = pltpu.VMEM((HEADS, ROWS), F32)
    names["lse"] = pltpu.VMEM((ROWS, HALF), F32)
    names["va"] = pltpu.VMEM((2, ROWS, C), BF)
    names["heads"] = pltpu.VMEM((2, ROWS, HALF), F32)
    names["slot"] = pltpu.VMEM((1, ROWS), jnp.int32)
    for name in ("place", "splace"):
        names[name] = pltpu.VMEM((PEERS, 8, ROOM), jnp.int32)
    for name in ("spts", "scot", "sres", "sgrad", "rpts", "rcot", "rres", "rgrad"):
        names[name] = pltpu.VMEM(room, BF)
    for name in ("place", "pts", "cot", "res", "grad"):
        names["send" + name] = sent((PEERS,))
        names["recv" + name] = sent((PEERS,))
    for name, outer, inner, wide, piece in (
        ("a", n_dp, PEERS, 2 * FF, (rows, HALF)),
        ("b", n_dp, PEERS, 2 * C, (rows // 4, HALF)),
        ("c", PEERS, n_dp, 2 * C, (C // PEERS // min(2, n_dp), 2 * C * min(2, n_dp) // n_dp)),
    ):
        for part in ("own", "got", "all"):
            names[name + part] = pltpu.VMEM((outer, C // outer, wide), BF)
        for part in ("cut", "cutgot", "fin"):
            names[name + part] = pltpu.VMEM((inner, *piece), F32)
        for step in range(4):
            names[f"{name}send{step}"] = sent((PEERS,))
            names[f"{name}recv{step}"] = sent((PEERS,))
    shapes = ((1, ROWS), tall, tall, (C, 3 * C), (C, C), (C, FF), (FF, C))
    for at, shape in enumerate(shapes):
        names[f"in{at}"] = pltpu.VMEM(shape, BF if at else jnp.int32)
    names["loaded"] = sent((7,))
    return names


class Scratch:
    def __init__(self, names, refs):
        for name, ref in zip(names, refs):
            setattr(self, name, ref)


def kernel(
    n_dp, names, tgt_in, pts_in, cot_in, qkv_in, out_in, up_in, down_in,
    res_out, grad_out, a_out, b_out, c_out, *refs,
):
    s = Scratch(names, refs)
    seq, zed = lax.axis_index("seq"), lax.axis_index("dp")
    tgt, pts, cot, w_qkv, w_out, w_up, w_down = (
        getattr(s, f"in{at}") for at in range(7)
    )
    loads = [
        pltpu.make_async_copy(source, target, s.loaded.at[at])
        for at, (source, target) in enumerate(
            (
                (tgt_in, tgt), (pts_in, pts), (cot_in, cot), (qkv_in, w_qkv),
                (out_in, w_out), (up_in, w_up), (down_in, w_down),
            )
        )
    ]
    for load in loads:
        load.start()
    barrier = pltpu.get_barrier_semaphore()
    for axis, size, me in (("seq", PEERS, seq), ("dp", n_dp, zed)):
        for d in range(1, size):
            pl.semaphore_signal(
                barrier,
                inc=1,
                device_id={axis: lax.rem(me + d, size)},
                device_id_type=pl.DeviceIdType.MESH,
            )

    def exchange(name, sign, source, target):
        return Copies(
            "seq", PEERS, seq, sign, lambda d, p: source.at[d], lambda d: target.at[d],
            getattr(s, "send" + name), getattr(s, "recv" + name),
        )

    go_place = exchange("place", 1, s.splace, s.place)
    go_pts = exchange("pts", 1, s.spts, s.rpts)
    go_cot = exchange("cot", 1, s.scot, s.rcot)
    go_res = exchange("res", -1, s.sres, s.rres)
    go_grad = exchange("grad", -1, s.sgrad, s.rgrad)

    loads[0].wait()
    slot, aux = slot_rows(tgt[...], seq)
    s.slot[...] = slot
    pl.semaphore_wait(barrier, PEERS - 1 + n_dp - 1)
    def pack(rows_ref, own_ref, sent_ref, go):
        for d in (4, 8, 12, 0):
            mine = one_hot(iota((4 * ROOM, ROWS), 0) + d * ROOM == slot)
            block = dot(mine, rows_ref[...]).astype(BF)
            for at in range(4):
                piece = block[at * ROOM : (at + 1) * ROOM]
                if d + at:
                    sent_ref[d + at] = piece
                    if go is not None:
                        go.start(d + at)
                else:
                    own_ref[0] = piece

    loads[1].wait()
    pack(pts, s.rpts, s.spts, go_pts)
    for d in (4, 8, 12, 0):
        found = dot_nt(aux, one_hot(iota((4 * ROOM, ROWS), 0) + d * ROOM == slot))
        places = jnp.where(
            found[2:3] > 0.5, found[0:1] * 32.0 + found[1:2], float(ROWS)
        ).astype(jnp.int32)
        for at in range(4):
            place = jnp.broadcast_to(places[:, at * ROOM : (at + 1) * ROOM], (8, ROOM))
            if d + at:
                s.splace[d + at] = place
                go_place.start(d + at)
            else:
                s.place[0] = place
    for load in loads[2:]:
        load.wait()
    pack(cot, s.rcot, s.scot, None)

    def send_back(go, rows_ref, mine_ref, theirs_ref):
        rows = rows_ref[...]
        for d in (4, 8, 12, 0):
            cols = [
                column_of(s.place[d + at, 0:1, :].astype(F32)).astype(jnp.int32) for at in range(4)
            ]
            mine = one_hot(iota((4 * ROOM, ROWS), 1) == jnp.concatenate(cols, axis=0))
            block = dot(mine, rows).astype(BF)
            for at in range(4):
                piece = block[at * ROOM : (at + 1) * ROOM]
                if d + at:
                    theirs_ref[d + at] = piece
                    go.start(d + at)
                else:
                    mine_ref[0] = piece

    go_place.arrived()
    go_pts.arrived()
    go_cot.start()
    place_rows(s, s.rpts, s.x)
    first_part(s, w_qkv)
    attend(s)
    for half in range(2):
        s.att[:, half * HALF : (half + 1) * HALF] = s.heads[half].astype(BF)
    s.ot[...] = transpose_bf(s.att[...])
    go_cot.arrived()
    place_rows(s, s.rcot, s.cot)
    feed_forward(s, w_out, w_up, w_down)
    send_back(go_res, s.out, s.rres, s.sres)

    along_seq, along_dp = ("seq", PEERS, seq), ("dp", n_dp, zed)
    wide = Reduction(s, "a", along_dp, along_seq)
    early = Reduction(s, "b", along_dp, along_seq)
    late = Reduction(s, "c", along_seq, along_dp)

    def put(ref, values, at):
        ref[:, :, at : at + values.shape[1]] = values.astype(BF).reshape(
            *ref.shape[0:2], values.shape[1]
        )

    put(s.aown, dot(transpose_bf(s.second[...]), s.gexp[...]), 0)
    put(s.aown, dot(transpose_bf(s.cot[...]), s.act[...]), FF)
    wide.step0()
    out_grad = dot(s.ot[...], s.hrows[...])
    put(s.bown, out_grad[:, 0:HALF], 3 * HALF)
    put(s.cown, out_grad[:, HALF:C], 3 * HALF)

    def put_heads(ref, half):
        at = slice(half * HALF, (half + 1) * HALF)
        s.dq[:, at] = transpose_bf(s.dqt[at, :])
        for part, rows in enumerate((s.dq[:, at], s.dk[:, at].astype(BF), s.dv[:, at].astype(BF))):
            put(ref, dot(s.first_t[...], rows), part * HALF)

    prepare_back(s)

    def half_way():
        put_heads(s.bown, 0)
        early.step0()
        wide.step2()

    attend_back(
        s,
        {3: wide.step1, 4: half_way, 5: wide.step3, 6: early.step1, 7: early.step2},
    )
    early.step3()
    put_heads(s.cown, 1)
    late.step0()
    g_first = dot_nt(s.dq[...], w_qkv[:, 0:C]) + dot_nt(s.dk[...].astype(BF), w_qkv[:, C : 2 * C])
    g_first = g_first + dot_nt(s.dv[...].astype(BF), w_qkv[:, 2 * C : 3 * C])
    normed, inverse = normalize(s.x[...].astype(F32))
    g_first = g_first.astype(BF).astype(F32)
    s.out[...] = (s.gh[...] + norm_back(normed, inverse, g_first)).astype(BF)
    send_back(go_grad, s.out, s.rgrad, s.sgrad)
    late.step1()
    late.step2()
    go_res.arrived()
    home_rows(s, s.rres, res_out)
    late.step3()
    wide.step4(a_out)
    early.step4(b_out)
    go_grad.arrived()
    home_rows(s, s.rgrad, grad_out)
    late.step4(c_out)
    for go in (go_place, go_pts, go_cot, go_res, go_grad):
        go.sent()


def finish_kernel(factor, res, grad, a, b, c, res_out, grad_out, g_qkv, g_out, g_up, g_down):
    res_out[...] = res[...]
    grad_out[...] = grad[...]
    g_up[...] = a[:, 0:FF].astype(F32) * factor
    for at in range(0, FF, C):
        g_down[at : at + C, :] = a[:, FF + at : FF + at + C].astype(F32).T * factor
    for half, ref in enumerate((b, c)):
        for part in range(3):
            at = part * C + half * HALF
            g_qkv[:, at : at + HALF] = ref[:, part * HALF : (part + 1) * HALF].astype(F32) * factor
        g_out[:, half * HALF : (half + 1) * HALF] = ref[:, 3 * HALF :].astype(F32) * factor


def body(points, targets, cotangent, w_qkv, w_out, w_up, w_down):
    n_dp = lax.axis_size("dp")
    factor = 1.0 / math.sqrt(points.shape[0] * n_dp * lax.axis_size("seq") * points.shape[1])
    names = scratch_of(n_dp)
    vmem = pl.BlockSpec(memory_space=pltpu.VMEM)
    rows_type = jax.ShapeDtypeStruct((ROWS, C), BF)
    gathered = pl.pallas_call(
        lambda *refs: kernel(n_dp, list(names), *refs),
        out_shape=[
            rows_type,
            rows_type,
            jax.ShapeDtypeStruct((C, 2 * FF), BF),
            jax.ShapeDtypeStruct((C, 2 * C), BF),
            jax.ShapeDtypeStruct((C, 2 * C), BF),
        ],
        in_specs=[pl.BlockSpec(memory_space=pltpu.HBM)] * 7,
        out_specs=[vmem] * 5,
        scratch_shapes=list(names.values()),
        compiler_params=pltpu.CompilerParams(
            vmem_limit_bytes=61 * 1024 * 1024, collective_id=0, has_side_effects=True
        ),
    )(targets, points[0], cotangent[0], w_qkv, w_out, w_up, w_down)
    result, grad_points, *grads = pl.pallas_call(
        lambda *refs: finish_kernel(factor, *refs),
        out_shape=[
            rows_type,
            rows_type,
            jax.ShapeDtypeStruct((C, 3 * C), F32),
            jax.ShapeDtypeStruct((C, C), F32),
            jax.ShapeDtypeStruct((C, FF), F32),
            jax.ShapeDtypeStruct((FF, C), F32),
        ],
        in_specs=[vmem] * 5,
        out_specs=[vmem] * 6,
    )(*gathered)
    return (result[None], grad_points[None], *grads)


def solution(mesh):
    return jax.shard_map(
        body,
        mesh=mesh,
        in_specs=(P("dp", "seq", None), P("dp", "seq"), P("dp", "seq", None), P(), P(), P(), P()),
        out_specs=(P("dp", "seq", None), P("dp", "seq", None), P(), P(), P(), P()),
        check_vma=False,
    )
```

```python
import math

import jax
import jax.numpy as jnp
from jax import lax
from jax.experimental import pallas as pl
from jax.experimental.pallas import tpu as pltpu
from jax.sharding import PartitionSpec as P

BF = jnp.bfloat16
F32 = jnp.float32
C = 256
HEADS = 16
DH = 16
FF = 1024
ROWS = 1024
PEERS = 16
ROOM = 128
SLOTS = PEERS * ROOM
BLK = 256
NB = ROWS // BLK
HALF = 128
EPS = 1e-05
GELU_A = 0.7978845608028654
GELU_B = 0.044715


def dot(left, right):
    return lax.dot_general(left, right, (((1,), (0,)), ((), ())), preferred_element_type=F32)


def dot_nt(left, right):
    return lax.dot_general(left, right, (((1,), (1,)), ((), ())), preferred_element_type=F32)


def iota(shape, axis):
    return lax.broadcasted_iota(jnp.int32, shape, axis)


def one_hot(cond):
    return jnp.where(cond, 1.0, 0.0).astype(BF)


def transpose_bf(values):
    return values.astype(F32).T.astype(BF)


def normalize(values):
    center = jnp.mean(values, axis=-1, keepdims=True)
    shifted = values - center
    inverse_std = lax.rsqrt(jnp.mean(shifted * shifted, axis=-1, keepdims=True) + EPS)
    return shifted * inverse_std, inverse_std


def norm_back(normed, inverse_std, upstream):
    return inverse_std * (
        upstream
        - jnp.mean(upstream, axis=-1, keepdims=True)
        - normed * jnp.mean(upstream * normed, axis=-1, keepdims=True)
    )


def gelu_pair(inputs):
    square = inputs * inputs
    tangent = jnp.tanh(GELU_A * (inputs + GELU_B * square * inputs))
    half = 0.5 * (1.0 + tangent)
    slopes = half + 0.5 * inputs * (1.0 - tangent * tangent) * GELU_A * (
        1.0 + 3.0 * GELU_B * square
    )
    return inputs * half, slopes


def column_of(row):
    return jnp.broadcast_to(row, (128, 128)).T[:, 0:1]


def slot_rows(targets, me):
    owner = lax.shift_right_logical(targets, 10)
    local = jnp.bitwise_and(targets, ROWS - 1)
    marks = iota((PEERS, ROWS), 0) == owner
    before = one_hot(iota((ROWS, ROWS), 0) < iota((ROWS, ROWS), 1))
    counts = dot(one_hot(marks), before)
    rank = jnp.sum(jnp.where(marks, counts, 0.0), axis=0, keepdims=True)
    slot = jnp.bitwise_and(owner - me, PEERS - 1) * ROOM + rank.astype(jnp.int32)
    part = iota((PEERS, ROWS), 0)
    aux = jnp.where(
        part == 0,
        lax.shift_right_logical(local, 5),
        jnp.where(part == 1, jnp.bitwise_and(local, 31), 1),
    )
    return slot, aux.astype(F32).astype(BF)


def home_rows(s, back, out_ref):
    rows = back[...].reshape(SLOTS, C)
    for block in range(ROWS // 128):
        at = slice(block * 128, (block + 1) * 128)
        col = column_of(s.slot[:, at].astype(F32)).astype(jnp.int32)
        out_ref[at, :] = dot(one_hot(iota((128, SLOTS), 1) == col), rows).astype(BF)


def place_rows(s, recv_ref, out_ref):
    recv = recv_ref[...].reshape(SLOTS, C)
    for block in range(NB):
        pieces = [
            one_hot(iota((BLK, ROOM), 0) + block * BLK == s.place[peer, 0:1, :])
            for peer in range(PEERS)
        ]
        out_ref[block * BLK : (block + 1) * BLK, :] = dot(
            jnp.concatenate(pieces, axis=1), recv
        ).astype(BF)


def first_part(s, w_ref):
    normed, _ = normalize(s.x[...].astype(F32))
    first = normed.astype(BF)
    s.first_t[...] = transpose_bf(first)
    qs = (dot(first, w_ref[:, 0:C]).astype(BF).astype(F32) * 0.25).astype(BF)
    k = dot(first, w_ref[:, C : 2 * C]).astype(BF)
    v = dot(first, w_ref[:, 2 * C : 3 * C]).astype(BF)
    s.q[...] = qs
    s.k[...] = k
    s.v[...] = v
    s.qt[...] = transpose_bf(qs)
    s.kt[...] = transpose_bf(k)
    for half in range(2):
        s.va[half, :, 0:HALF] = v[:, half * HALF : (half + 1) * HALF]
        s.va[half, :, HALF:C] = jnp.ones((ROWS, HALF), BF)
    s.za[...] = jnp.zeros((C, ROWS), BF)


def head_rows(h):
    return pl.ds(pl.multiple_of(h * DH, DH), DH)


def only_head(h, zeroed_ref, rows):
    zeroed_ref[head_rows(jnp.maximum(h - 1, 0)), :] = jnp.zeros((DH, ROWS), BF)
    zeroed_ref[head_rows(h), :] = rows


def attend(s):
    @pl.loop(0, HEADS, unroll=2)
    def _(h):
        half = h // 8
        only_head(h, s.za, s.kt[head_rows(h), :])
        lane = iota((HALF, HALF), 1)
        for block in range(ROWS // HALF):
            rows = slice(block * HALF, (block + 1) * HALF)
            scores = dot(s.q[rows, :], s.za[...])
            top = jnp.max(scores, axis=1, keepdims=True)
            out = dot(jnp.exp(scores - top).astype(BF), s.va[half])
            total = out[:, HALF : HALF + 1]
            s.heads[half, rows, :] = jnp.where(
                lax.shift_right_logical(lane, 4) == h - 8 * half,
                out[:, 0:HALF] * (1.0 / total),
                s.heads[half, rows, :],
            )
            s.lse[rows, :] = jnp.where(lane == h, top + jnp.log(total), s.lse[rows, :])


def feed_forward(s, w_out, w_up, w_down):
    @pl.loop(0, NB)
    def _(block):
        rows = pl.ds(pl.multiple_of(block * BLK, BLK), BLK)
        features = s.x[rows, :].astype(F32)
        tile_grad = s.cot[rows, :]
        hidden = features + dot(s.att[rows, :], w_out[...])
        normed, inverse = normalize(hidden)
        second = normed.astype(BF)
        s.second[rows, :] = second
        expanded = dot(second, w_up[...])
        activated, slopes = gelu_pair(expanded)
        activated = activated.astype(BF)
        s.act[rows, :] = activated
        s.out[rows, :] = (hidden + dot(activated, w_down[...])).astype(BF)
        gexp = (dot_nt(tile_grad, w_down[...]) * slopes).astype(BF)
        s.gexp[rows, :] = gexp
        grad_hidden = tile_grad.astype(F32) + norm_back(normed, inverse, dot_nt(gexp, w_up[...]))
        s.gh[rows, :] = grad_hidden
        hrows = grad_hidden.astype(BF)
        s.hrows[rows, :] = hrows
        s.datt[rows, :] = dot_nt(hrows, w_out[...]).astype(BF)


def prepare_back(s):
    dot_t = s.datt[...].astype(F32).T
    s.dot_t[...] = dot_t.astype(BF)
    inner = (dot_t * s.ot[...].astype(F32)).reshape(HEADS, DH, ROWS)
    s.inner[...] = jnp.sum(inner, axis=1, keepdims=True).reshape(HEADS, ROWS)
    s.lse_t[...] = s.lse[...].T[0:HEADS]
    s.za[...] = jnp.zeros((C, ROWS), BF)
    s.zb[...] = jnp.zeros((C, ROWS), BF)


def attend_back(s, steps):
    @pl.loop(0, HEADS // 2)
    def _(pair):
        for when, step in steps.items():
            pl.when(pair == when)(step)
        for odd in range(2):
            head_back(s, pair * 2 + odd)


def head_back(s, h):
    only_head(h, s.za, s.qt[head_rows(h), :])
    only_head(h, s.zb, s.dot_t[head_rows(h), :])
    keys = s.kt[head_rows(h), :]
    for block in range(NB):
        cols = slice(block * BLK, (block + 1) * BLK)
        probs = jnp.exp(dot(s.k[...], s.za[:, cols]) - s.lse_t[pl.ds(h, 1), cols])
        dp = dot(s.v[...], s.zb[:, cols])
        ds = (probs * (dp - s.inner[pl.ds(h, 1), cols])).astype(BF)
        s.p[:, cols] = probs.astype(BF)
        s.ds[:, cols] = ds
        s.dqt[head_rows(h), cols] = (dot(keys, ds) * 0.25).astype(BF)
    mine = lax.shift_right_logical(iota((ROWS, C), 1), 4) == h
    s.dv[...] = jnp.where(mine, dot(s.p[...], s.datt[...]), s.dv[...])
    s.dk[...] = jnp.where(mine, dot(s.ds[...], s.q[...]), s.dk[...])


class Copies:
    def __init__(self, axis, size, me, sign, source, target, send, recv):
        self.parts = {}
        for d in range(1, size):
            peer = lax.rem(me + (d if sign > 0 else size - d), size)
            self.parts[d] = pltpu.make_async_remote_copy(
                src_ref=source(d, peer),
                dst_ref=target(d),
                send_sem=send.at[d],
                recv_sem=recv.at[d],
                device_id={axis: peer},
                device_id_type=pl.DeviceIdType.MESH,
            )

    def start(self, d=None):
        for key, part in self.parts.items():
            if d is None or key == d:
                part.start()

    def arrived(self):
        for part in self.parts.values():
            part.wait_recv()

    def sent(self):
        for part in self.parts.values():
            part.wait_send()


class Reduction:
    def __init__(self, s, name, outer, inner):
        self.outer, self.inner = outer, inner
        self.own, self.got, self.cut, self.cut_got, self.fin, self.all = (
            getattr(s, name + part) for part in ("own", "got", "cut", "cutgot", "fin", "all")
        )
        sems = [(getattr(s, f"{name}send{i}"), getattr(s, f"{name}recv{i}")) for i in range(4)]
        at, to = outer[2], inner[2]
        self.first = lambda: Copies(
            *outer, 1, lambda d, p: self.own.at[p], lambda d: self.got.at[d], *sems[0]
        )
        self.second = lambda: Copies(
            *inner, 1, lambda d, p: self.cut.at[p], lambda d: self.cut_got.at[d], *sems[1]
        )
        self.third = lambda: Copies(
            *inner, 1, lambda d, p: self.fin.at[to], lambda d: self.fin.at[to], *sems[2]
        )
        self.fourth = lambda: Copies(
            *outer, 1, lambda d, p: self.all.at[at], lambda d: self.all.at[at], *sems[3]
        )

    def spots(self):
        rows, cols = self.cut.shape[1:]
        across = self.own.shape[2] // cols
        for piece in range(self.inner[1]):
            up, along = piece // across, piece % across
            yield piece, slice(up * rows, (up + 1) * rows), slice(along * cols, (along + 1) * cols)

    def step0(self):
        self.first().start()

    def step1(self):
        self.first().arrived()
        for piece, rows, cols in self.spots():
            total = self.own[self.outer[2], rows, cols].astype(F32)
            for d in range(1, self.outer[1]):
                total = total + self.got[d, rows, cols].astype(F32)
            self.cut[piece] = total
        self.second().start()

    def step2(self):
        self.second().arrived()
        total = self.cut[self.inner[2]]
        for d in range(1, self.inner[1]):
            total = total + self.cut_got[d]
        self.fin[self.inner[2]] = total
        self.third().start()

    def step3(self):
        self.third().arrived()
        across = self.own.shape[2] // self.cut.shape[2]
        bands = [
            jnp.concatenate([self.fin[at + piece] for piece in range(across)], axis=1)
            for at in range(0, self.inner[1], across)
        ]
        self.all[self.outer[2]] = jnp.concatenate(bands, axis=0).astype(BF)
        self.fourth().start()

    def step4(self, out_ref):
        self.fourth().arrived()
        out_ref[...] = self.all[...].reshape(out_ref.shape)
        for copies in (self.first, self.second, self.third, self.fourth):
            copies().sent()


class ShortReduction:
    def __init__(self, s, name, seq, zed, n_dp):
        self.seq, self.zed, self.n_dp = seq, zed, n_dp
        self.own, self.got, self.mid, self.all = (
            getattr(s, name + part) for part in ("own", "got", "mid", "all")
        )
        sems = [(getattr(s, f"{name}send{i}"), getattr(s, f"{name}recv{i}")) for i in range(3)]
        self.first = lambda: Copies(
            "seq", PEERS, seq, 1, lambda d, p: self.own.at[p], lambda d: self.got.at[d], *sems[0]
        )
        self.second = lambda: Copies(
            "dp", n_dp, zed, 1, lambda d, p: self.mid.at[zed], lambda d: self.mid.at[zed], *sems[1]
        )
        self.third = lambda: Copies(
            "seq", PEERS, seq, 1, lambda d, p: self.all.at[seq], lambda d: self.all.at[seq], *sems[2]
        )

    def step0(self):
        self.first().start()

    def step1(self):
        self.first().arrived()
        total = self.own[self.seq].astype(F32)
        for d in range(1, PEERS):
            total = total + self.got[d].astype(F32)
        self.mid[self.zed] = total.astype(BF)
        self.second().start()

    def step2(self):
        self.second().arrived()
        total = self.mid[0].astype(F32)
        for other in range(1, self.n_dp):
            total = total + self.mid[other].astype(F32)
        self.all[self.seq] = total.astype(BF)
        self.third().start()

    def step3(self, out_ref):
        self.third().arrived()
        out_ref[...] = self.all[...].reshape(out_ref.shape)
        for copies in (self.first, self.second, self.third):
            copies().sent()


def scratch_of(n_dp):
    rows = C // n_dp
    room, tall, flat, sent = (PEERS, ROOM, C), (ROWS, C), (C, ROWS), pltpu.SemaphoreType.DMA
    names = {}
    for name in ("x", "cot", "dq", "q", "k", "v", "att", "second", "hrows", "datt", "out"):
        names[name] = pltpu.VMEM(tall, BF)
    for name in ("gh", "dv", "dk"):
        names[name] = pltpu.VMEM(tall, F32)
    for name in ("first_t", "qt", "kt", "za", "zb", "ot", "dot_t", "dqt"):
        names[name] = pltpu.VMEM(flat, BF)
    for name in ("act", "gexp", "p", "ds"):
        names[name] = pltpu.VMEM((ROWS, FF), BF)
    for name in ("inner", "lse_t"):
        names[name] = pltpu.VMEM((HEADS, ROWS), F32)
    names["lse"] = pltpu.VMEM((ROWS, HALF), F32)
    names["va"] = pltpu.VMEM((2, ROWS, C), BF)
    names["heads"] = pltpu.VMEM((2, ROWS, HALF), F32)
    names["slot"] = pltpu.VMEM((1, ROWS), jnp.int32)
    for name in ("place", "splace"):
        names[name] = pltpu.VMEM((PEERS, 8, ROOM), jnp.int32)
    for name in ("spts", "scot", "sres", "sgrad", "rpts", "rcot", "rres", "rgrad"):
        names[name] = pltpu.VMEM(room, BF)
    for name in ("place", "pts", "cot", "res", "grad"):
        names["send" + name] = sent((PEERS,))
        names["recv" + name] = sent((PEERS,))
    for name, outer, inner, wide, piece in (
        ("a", n_dp, PEERS, 2 * FF, (rows, HALF)),
        ("b", n_dp, PEERS, 2 * C, (rows // 4, HALF)),
    ):
        for part in ("own", "got", "all"):
            names[name + part] = pltpu.VMEM((outer, C // outer, wide), BF)
        for part in ("cut", "cutgot", "fin"):
            names[name + part] = pltpu.VMEM((inner, *piece), F32)
        for step in range(4):
            names[f"{name}send{step}"] = sent((PEERS,))
            names[f"{name}recv{step}"] = sent((PEERS,))
    for part in ("own", "got", "all"):
        names["c" + part] = pltpu.VMEM((PEERS, C // PEERS, 2 * C), BF)
    names["cmid"] = pltpu.VMEM((n_dp, C // PEERS, 2 * C), BF)
    for step in range(3):
        names[f"csend{step}"] = sent((PEERS,))
        names[f"crecv{step}"] = sent((PEERS,))
    return names


class Scratch:
    def __init__(self, names, refs):
        for name, ref in zip(names, refs):
            setattr(self, name, ref)


def kernel(
    n_dp, names, tgt, pts, cot, w_qkv, w_out, w_up, w_down,
    res_out, grad_out, a_out, b_out, c_out, *refs,
):
    s = Scratch(names, refs)
    seq, zed = lax.axis_index("seq"), lax.axis_index("dp")
    barrier = pltpu.get_barrier_semaphore()
    for axis, size, me in (("seq", PEERS, seq), ("dp", n_dp, zed)):
        for d in range(1, size):
            pl.semaphore_signal(
                barrier,
                inc=1,
                device_id={axis: lax.rem(me + d, size)},
                device_id_type=pl.DeviceIdType.MESH,
            )

    def exchange(name, sign, source, target):
        return Copies(
            "seq", PEERS, seq, sign, lambda d, p: source.at[d], lambda d: target.at[d],
            getattr(s, "send" + name), getattr(s, "recv" + name),
        )

    go_place = exchange("place", 1, s.splace, s.place)
    go_pts = exchange("pts", 1, s.spts, s.rpts)
    go_cot = exchange("cot", 1, s.scot, s.rcot)
    go_res = exchange("res", -1, s.sres, s.rres)
    go_grad = exchange("grad", -1, s.sgrad, s.rgrad)

    slot, aux = slot_rows(tgt[...], seq)
    s.slot[...] = slot
    pl.semaphore_wait(barrier, PEERS - 1 + n_dp - 1)
    def pack(rows_ref, own_ref, sent_ref, go):
        for d in (4, 8, 12, 0):
            mine = one_hot(iota((4 * ROOM, ROWS), 0) + d * ROOM == slot)
            block = dot(mine, rows_ref[...]).astype(BF)
            for at in range(4):
                piece = block[at * ROOM : (at + 1) * ROOM]
                if d + at:
                    sent_ref[d + at] = piece
                    if go is not None:
                        go.start(d + at)
                else:
                    own_ref[0] = piece

    pack(pts, s.rpts, s.spts, go_pts)
    for d in (4, 8, 12, 0):
        found = dot_nt(aux, one_hot(iota((4 * ROOM, ROWS), 0) + d * ROOM == slot))
        places = jnp.where(
            found[2:3] > 0.5, found[0:1] * 32.0 + found[1:2], float(ROWS)
        ).astype(jnp.int32)
        for at in range(4):
            place = jnp.broadcast_to(places[:, at * ROOM : (at + 1) * ROOM], (8, ROOM))
            if d + at:
                s.splace[d + at] = place
                go_place.start(d + at)
            else:
                s.place[0] = place
    pack(cot, s.rcot, s.scot, None)

    def send_back(go, rows_ref, mine_ref, theirs_ref):
        rows = rows_ref[...]
        for d in (4, 8, 12, 0):
            cols = [
                column_of(s.place[d + at, 0:1, :].astype(F32)).astype(jnp.int32) for at in range(4)
            ]
            mine = one_hot(iota((4 * ROOM, ROWS), 1) == jnp.concatenate(cols, axis=0))
            block = dot(mine, rows).astype(BF)
            for at in range(4):
                piece = block[at * ROOM : (at + 1) * ROOM]
                if d + at:
                    theirs_ref[d + at] = piece
                    go.start(d + at)
                else:
                    mine_ref[0] = piece

    go_place.arrived()
    go_pts.arrived()
    go_cot.start()
    place_rows(s, s.rpts, s.x)
    first_part(s, w_qkv)
    attend(s)
    for half in range(2):
        s.att[:, half * HALF : (half + 1) * HALF] = s.heads[half].astype(BF)
    s.ot[...] = transpose_bf(s.att[...])
    go_cot.arrived()
    place_rows(s, s.rcot, s.cot)
    feed_forward(s, w_out, w_up, w_down)
    send_back(go_res, s.out, s.rres, s.sres)

    along_seq, along_dp = ("seq", PEERS, seq), ("dp", n_dp, zed)
    wide = Reduction(s, "a", along_dp, along_seq)
    early = Reduction(s, "b", along_dp, along_seq)
    late = ShortReduction(s, "c", seq, zed, n_dp)

    def put(ref, values, at):
        ref[:, :, at : at + values.shape[1]] = values.astype(BF).reshape(
            *ref.shape[0:2], values.shape[1]
        )

    put(s.aown, dot(transpose_bf(s.second[...]), s.gexp[...]), 0)
    put(s.aown, dot(transpose_bf(s.cot[...]), s.act[...]), FF)
    wide.step0()
    out_grad = dot(s.ot[...], s.hrows[...])
    put(s.bown, out_grad[:, 0:HALF], 3 * HALF)
    put(s.cown, out_grad[:, HALF:C], 3 * HALF)

    def put_heads(ref, half):
        at = slice(half * HALF, (half + 1) * HALF)
        s.dq[:, at] = transpose_bf(s.dqt[at, :])
        for part, rows in enumerate((s.dq[:, at], s.dk[:, at].astype(BF), s.dv[:, at].astype(BF))):
            put(ref, dot(s.first_t[...], rows), part * HALF)

    prepare_back(s)

    def half_way():
        put_heads(s.bown, 0)
        early.step0()
        wide.step3()

    attend_back(
        s,
        {
            2: wide.step1,
            3: wide.step2,
            4: half_way,
            5: early.step1,
            6: early.step2,
            7: early.step3,
        },
    )
    put_heads(s.cown, 1)
    late.step0()
    g_first = dot_nt(s.dq[...], w_qkv[:, 0:C]) + dot_nt(s.dk[...].astype(BF), w_qkv[:, C : 2 * C])
    g_first = g_first + dot_nt(s.dv[...].astype(BF), w_qkv[:, 2 * C : 3 * C])
    normed, inverse = normalize(s.x[...].astype(F32))
    g_first = g_first.astype(BF).astype(F32)
    s.out[...] = (s.gh[...] + norm_back(normed, inverse, g_first)).astype(BF)
    late.step1()
    send_back(go_grad, s.out, s.rgrad, s.sgrad)
    go_res.arrived()
    home_rows(s, s.rres, res_out)
    late.step2()
    wide.step4(a_out)
    early.step4(b_out)
    go_grad.arrived()
    home_rows(s, s.rgrad, grad_out)
    late.step3(c_out)
    for go in (go_place, go_pts, go_cot, go_res, go_grad):
        go.sent()


def finish_kernel(factor, res, grad, a, b, c, res_out, grad_out, g_qkv, g_out, g_up, g_down):
    res_out[...] = res[...]
    grad_out[...] = grad[...]
    g_up[...] = a[:, 0:FF].astype(F32) * factor
    for at in range(0, FF, C):
        g_down[at : at + C, :] = a[:, FF + at : FF + at + C].astype(F32).T * factor
    for half, ref in enumerate((b, c)):
        for part in range(3):
            at = part * C + half * HALF
            g_qkv[:, at : at + HALF] = ref[:, part * HALF : (part + 1) * HALF].astype(F32) * factor
        g_out[:, half * HALF : (half + 1) * HALF] = ref[:, 3 * HALF :].astype(F32) * factor


def body(points, targets, cotangent, w_qkv, w_out, w_up, w_down):
    n_dp = lax.axis_size("dp")
    factor = 1.0 / math.sqrt(points.shape[0] * n_dp * lax.axis_size("seq") * points.shape[1])
    names = scratch_of(n_dp)
    vmem = pl.BlockSpec(memory_space=pltpu.VMEM)
    rows_type = jax.ShapeDtypeStruct((ROWS, C), BF)
    gathered = pl.pallas_call(
        lambda *refs: kernel(n_dp, list(names), *refs),
        out_shape=[
            rows_type,
            rows_type,
            jax.ShapeDtypeStruct((C, 2 * FF), BF),
            jax.ShapeDtypeStruct((C, 2 * C), BF),
            jax.ShapeDtypeStruct((C, 2 * C), BF),
        ],
        in_specs=[vmem] * 7,
        out_specs=[vmem] * 5,
        scratch_shapes=list(names.values()),
        compiler_params=pltpu.CompilerParams(
            vmem_limit_bytes=60 * 1024 * 1024, collective_id=0, has_side_effects=True
        ),
    )(targets, points[0], cotangent[0], w_qkv, w_out, w_up, w_down)
    result, grad_points, *grads = pl.pallas_call(
        lambda *refs: finish_kernel(factor, *refs),
        out_shape=[
            rows_type,
            rows_type,
            jax.ShapeDtypeStruct((C, 3 * C), F32),
            jax.ShapeDtypeStruct((C, C), F32),
            jax.ShapeDtypeStruct((C, FF), F32),
            jax.ShapeDtypeStruct((FF, C), F32),
        ],
        in_specs=[vmem] * 5,
        out_specs=[vmem] * 6,
    )(*gathered)
    return (result[None], grad_points[None], *grads)


def solution(mesh):
    return jax.shard_map(
        body,
        mesh=mesh,
        in_specs=(P("dp", "seq", None), P("dp", "seq"), P("dp", "seq", None), P(), P(), P(), P()),
        out_specs=(P("dp", "seq", None), P("dp", "seq", None), P(), P(), P(), P()),
        check_vma=False,
    )
```
